128 devices in a mesh: wide: 32 (over x, z, core), narrow: 4 (over y).
Axes of the slice: x: 4, y: 4, z: 4, core: 2. Of those that a mesh axis runs over, the one named last changes fastest.
Arguments:
- member: bfloat16 [2048, 8192], P('narrow', 'wide'), may hold values from 0.01 to 300, as said below
Outputs:
- transition: float32 [8192, 8192], P('wide', 'narrow')
- stationary: float32 [8192], P('wide')
The draws below stay inside these ranges and needn't reach their ends.
Inputs may be any that keep to these rules, and one draw needn't show every extreme that they name: `member`: strictly positive weights.
All inputs are finite; a program needn't handle non-finite values.
Results may differ from the reference program's by a relative error of at most 0.0003.
Values may be sent and summed in bfloat16 or wider, within the bound.
No kernel may reach another device: no remote copies, remote signals or barrier semaphores. Data moves between devices by JAX's collectives and lax.ppermute only.
A program may use at most 128 MiB of HBM per device.

```python
import math
import jax
import jax.numpy as jnp

STATES = 8192
TAU = 64
ITERS = 3
FRAMES = 2048


def draw_member(key, part):
    key_base, key_state, key_phase, key_second = jax.random.split(key, 4)
    frame_idx = jnp.arange(FRAMES, dtype=jnp.float32)
    frame_pos = frame_idx / (FRAMES - 1)
    state_pos = jnp.arange(STATES, dtype=jnp.float32) / (STATES - 1)
    base = jnp.exp(jax.random.uniform(key_base, (FRAMES, STATES), jnp.float32, math.log(0.1), 0.0))
    state_scale = jnp.exp(jax.random.uniform(key_state, (STATES,), jnp.float32, 0.0, math.log(10.0)))
    phase = math.pi * state_pos + jax.random.uniform(key_phase, (STATES,), jnp.float32, -0.5, 0.5)
    second = jax.random.uniform(key_second, (STATES,), jnp.float32, -math.pi, math.pi)
    slow_angle = 2.0 * math.pi / (4.0 * TAU) * frame_idx
    fast_angle = 2.0 * math.pi / (2.0 * TAU) * frame_idx
    slow = 1.0 + 0.8 * jnp.sin(slow_angle[:, None] + phase[None, :])
    fast = 1.0 + 0.4 * jnp.sin(fast_angle[:, None] + second[None, :])
    value = base * (state_scale * (1.0 + 2.0 * state_pos))[None, :]
    value = value * (1.0 + 2.0 * frame_pos)[:, None]
    value = value * slow * fast
    return value.astype(jnp.bfloat16)


def setup_inputs(seed: int = 0) -> dict:
    key_list = jax.random.split(jax.random.key(seed), 2)
    member = draw_member(jax.random.fold_in(key_list[1], 71), 0)
    return dict(member=member)


def reference(member):
    lead = member[:FRAMES - TAU]
    lagged = member[TAU:]
    counts_raw = jnp.dot(lead.T, lagged, preferred_element_type=jnp.float32)
    sym = counts_raw + counts_raw.T
    visits = jnp.sum(counts_raw, axis=1)
    estimate = sym
    totals = jnp.sum(estimate, axis=1)
    for step in range(ITERS):
        ratio = visits / totals
        estimate = sym / (ratio[:, None] + ratio[None, :])
        totals = jnp.sum(estimate, axis=1)
    transition = STATES * estimate / totals[:, None]
    stationary = STATES * totals / jnp.sum(totals)
    return transition, stationary
```

```python
import jax
import jax.numpy as jnp
from jax import lax
from jax.experimental import pallas as pl
from jax.experimental.pallas import tpu as pltpu
from jax.sharding import Mesh, PartitionSpec as P

STATES = 8192
TAU = 64
ITERS = 3
FRAMES = 2048
WIDE = ("x", "z", "c")
ALL = ("x", "z", "c", "y")
BLOCK = 512
WIDTH = 256
COLS = 2048
GROUPS = COLS // WIDTH


def place(x, y, z, c):
    return ((x * 4 + z) * 2 + c) * 4 + y


def across():
    return [
        (place(x, y, z, c), place(y, x, z, c))
        for x in range(4) for y in range(4) for z in range(4) for c in range(2)
    ]


def along(k):
    return [(i, (i + k) % 4) for i in range(4)]


def to_all(values):
    sent = jnp.broadcast_to(values[None], (128,) + values.shape)
    got = lax.all_to_all(sent, ALL, 0, 0)
    return got.reshape((32, 4) + values.shape)


def multiply(rows_t, weights, piece):
    def kernel(rows_ref, weight_ref, piece_ref, sym_ref, col_ref, row_ref):
        g = pl.program_id(0)

        @pl.when(g == 0)
        def _():
            row_ref[...] = lax.dot_general(
                weight_ref[...], rows_ref[:, TAU:TAU + FRAMES],
                (((1,), (1,)), ((), ())), preferred_element_type=jnp.float32)

        acc = jnp.zeros((WIDTH, WIDTH), jnp.float32)
        col = jnp.zeros((16, WIDTH), jnp.float32)
        for q in range(4):
            block = piece_ref[q, 0]
            lo = q * BLOCK
            acc += jnp.dot(rows_ref[:, lo:lo + BLOCK], block, preferred_element_type=jnp.float32)
            acc += jnp.dot(rows_ref[:, lo + 2 * TAU:lo + 2 * TAU + BLOCK], block,
                           preferred_element_type=jnp.float32)
            col += jnp.dot(weight_ref[:, lo:lo + BLOCK], block, preferred_element_type=jnp.float32)
        sym_ref[...] = acc
        col_ref[...] = col

    return pl.pallas_call(
        kernel,
        grid=(GROUPS,),
        in_specs=[
            pl.BlockSpec((WIDTH, FRAMES + 2 * TAU), lambda g: (0, 0)),
            pl.BlockSpec((16, FRAMES), lambda g: (0, 0)),
            pl.BlockSpec((4, 1, BLOCK, WIDTH), lambda g: (0, g, 0, 0)),
        ],
        out_specs=[
            pl.BlockSpec((WIDTH, WIDTH), lambda g: (0, g)),
            pl.BlockSpec((16, WIDTH), lambda g: (0, g)),
            pl.BlockSpec((16, WIDTH), lambda g: (0, 0)),
        ],
        out_shape=[
            jax.ShapeDtypeStruct((WIDTH, COLS), jnp.float32),
            jax.ShapeDtypeStruct((16, COLS), jnp.float32),
            jax.ShapeDtypeStruct((16, WIDTH), jnp.float32),
        ],
    )(rows_t, weights, piece)


def three_parts(v):
    hi = v.astype(jnp.bfloat16)
    rest = v - hi.astype(jnp.float32)
    mid = rest.astype(jnp.bfloat16)
    lo = (rest - mid.astype(jnp.float32)).astype(jnp.bfloat16)
    return [hi, mid, lo]


def own_rows(member):
    y = lax.axis_index("y")
    later = [lax.ppermute(member, "y", along(-k)) for k in (1, 2, 3)]
    turned = jnp.concatenate([member] + later, axis=0).T
    rows = jnp.roll(turned, y * BLOCK, axis=1)
    return jnp.pad(rows, ((0, 0), (TAU, TAU)))


def shards(member):
    y = lax.axis_index("y")
    w = (lax.axis_index("x") * 4 + lax.axis_index("z")) * 2 + lax.axis_index("c")
    moved = lax.ppermute(member, ALL, across())
    piece = lax.all_gather(moved, WIDE, axis=0).reshape(4, GROUPS, BLOCK, WIDTH)
    rows_t = own_rows(member)
    part = jnp.sum(member, axis=1, dtype=jnp.float32)
    frame = jnp.sum(to_all(part), axis=0).reshape(FRAMES)
    up = jnp.pad(frame[TAU:], (0, TAU))
    down = jnp.pad(frame[:FRAMES - TAU], (TAU, 0))
    weights = jnp.stack(three_parts(up) + three_parts(down))
    weights = jnp.pad(weights, ((0, 10), (0, 0)))
    sym, col_sums, row_sums = multiply(rows_t, weights, piece)
    visit_rows = jnp.sum(row_sums[:3], axis=0)
    total_rows = jnp.sum(row_sums[:6], axis=0)
    visit_cols = jnp.sum(col_sums[:3], axis=0)
    total_cols = jnp.sum(col_sums[:6], axis=0)
    for step in range(ITERS):
        ratio_rows = visit_rows / total_rows
        ratio_cols = visit_cols / total_cols
        estimate = sym / (ratio_rows[:, None] + ratio_cols[None, :])
        totals = jnp.sum(to_all(jnp.sum(estimate, axis=1)), axis=1).reshape(STATES)
        total_rows = lax.dynamic_slice_in_dim(totals, w * WIDTH, WIDTH)
        total_cols = lax.dynamic_slice_in_dim(totals, y * COLS, COLS)
    transition = STATES * estimate / total_rows[:, None]
    stationary = STATES * total_rows / jnp.sum(totals)
    return (transition, stationary)


def solution(mesh):
    mesh = Mesh(mesh.devices.reshape(4, 4, 2, 4), ALL)
    return jax.shard_map(
        shards,
        mesh=mesh,
        in_specs=(P("y", WIDE),),
        out_specs=(P(WIDE, "y"), P(WIDE)),
        check_vma=False,
    )
```

```python
import jax
import jax.numpy as jnp
from jax import lax
from jax.experimental import pallas as pl
from jax.experimental.pallas import tpu as pltpu
from jax.sharding import Mesh, PartitionSpec as P

STATES = 8192
TAU = 64
ITERS = 3
FRAMES = 2048
WIDE = ("x", "z", "c")
ALL = ("x", "z", "c", "y")
BLOCK = 512
WIDTH = 256
COLS = 2048
FIRST = 256


def place(x, y, z, c):
    return ((x * 4 + z) * 2 + c) * 4 + y


def across():
    return [
        (place(x, y, z, c), place(y, x, z, c))
        for x in range(4) for y in range(4) for z in range(4) for c in range(2)
    ]


def along(k):
    return [(i, (i + k) % 4) for i in range(4)]


def to_all(values):
    sent = jnp.broadcast_to(values[None], (128,) + values.shape)
    got = lax.all_to_all(sent, ALL, 0, 0)
    return got.reshape((32, 4) + values.shape)


def multiply(where, rows_t, weights, by_x, by_z, half, before):
    first = by_x[0].shape[1]

    def kernel(where_ref, rows_ref, weight_ref, *refs):
        x_refs, z_refs = refs[:4], refs[4:8]
        sym_ref, col_ref = refs[-2:]
        for dz in range(4):
            @pl.when(pl.program_id(0) == dz)
            def _(dz=dz):
                acc = jnp.zeros((WIDTH, WIDTH), jnp.float32)
                col = jnp.zeros((16, WIDTH), jnp.float32)
                for dx in range(4):
                    lo = pl.multiple_of(lax.rem(where_ref[0] + 4 - dx, 4) * BLOCK, BLOCK)
                    block = jnp.concatenate([x_refs[dx][dz], z_refs[dz][dx]], axis=0)
                    acc += jnp.dot(rows_ref[:, pl.ds(lo, BLOCK)], block,
                                   preferred_element_type=jnp.float32)
                    acc += jnp.dot(rows_ref[:, pl.ds(lo + 2 * TAU, BLOCK)], block,
                                   preferred_element_type=jnp.float32)
                    col += jnp.dot(weight_ref[:, pl.ds(lo, BLOCK)], block,
                                   preferred_element_type=jnp.float32)
                sym_ref[...] = acc
                col_ref[...] = col

    def group(g, w):
        return (0, lax.rem(w[1] + 4 - g, 4) * 2 + (w[2] if half == 0 else 1 - w[2]))

    whole = lambda shape: pl.BlockSpec(shape, lambda g, w: (0,) * len(shape))
    in_specs = [whole(rows_t.shape), whole(weights.shape)]
    in_specs += [whole(v.shape) for v in by_x + by_z]
    operands = [where, rows_t, weights] + by_x + by_z
    aliases = {}
    if before is not None:
        in_specs += [pl.BlockSpec(memory_space=pl.ANY)] * 2
        aliases = {len(operands): 0, len(operands) + 1: 1}
        operands += list(before)
    return pl.pallas_call(
        kernel,
        grid_spec=pltpu.PrefetchScalarGridSpec(
            num_scalar_prefetch=1,
            grid=(4,),
            in_specs=in_specs,
            out_specs=[pl.BlockSpec((WIDTH, WIDTH), group), pl.BlockSpec((16, WIDTH), group)],
        ),
        out_shape=[
            jax.ShapeDtypeStruct((WIDTH, COLS), jnp.float32),
            jax.ShapeDtypeStruct((16, COLS), jnp.float32),
        ],
        input_output_aliases=aliases,
    )(*operands)


def three_parts(v):
    hi = v.astype(jnp.bfloat16)
    rest = v - hi.astype(jnp.float32)
    mid = rest.astype(jnp.bfloat16)
    lo = (rest - mid.astype(jnp.float32)).astype(jnp.bfloat16)
    return [hi, mid, lo]


def own_rows(member):
    y = lax.axis_index("y")
    later = [lax.ppermute(member, "y", along(-k)) for k in (1, 2, 3)]
    turned = jnp.concatenate([member] + later, axis=0).T
    rows = jnp.roll(turned, y * BLOCK, axis=1)
    return jnp.pad(rows, ((0, 0), (TAU, TAU)))


def ring(v, axis):
    return [v] + [lax.ppermute(v, axis, along(k)) for k in (1, 2, 3)]


def shards(member):
    y = lax.axis_index("y")
    x, z, c = lax.axis_index("x"), lax.axis_index("z"), lax.axis_index("c")
    w = (x * 4 + z) * 2 + c
    where = jnp.stack([x, z, c])
    moved = lax.ppermute(member, ALL, across())
    by_x = ring(jnp.stack(ring(moved[:FIRST], "z")), "x")
    by_z = ring(jnp.stack(ring(moved[FIRST:], "x")), "z")
    swap = [(0, 1), (1, 0)]
    other_x = [lax.ppermute(v, "c", swap) for v in by_x]
    other_z = [lax.ppermute(v, "c", swap) for v in by_z]
    rows_t = own_rows(member)
    part = jnp.sum(member, axis=1, dtype=jnp.float32)
    frame = jnp.sum(to_all(part), axis=0).reshape(FRAMES)
    up = jnp.pad(frame[TAU:], (0, TAU))
    down = jnp.pad(frame[:FRAMES - TAU], (TAU, 0))
    weights = jnp.stack(three_parts(up) + three_parts(down))
    weights = jnp.pad(weights, ((0, 10), (0, 0)))
    row_sums = lax.dot_general(
        weights, rows_t[:, TAU:TAU + FRAMES], (((1,), (1,)), ((), ())),
        preferred_element_type=jnp.float32)
    own = multiply(where, rows_t, weights, by_x, by_z, 0, None)
    sym, col_sums = multiply(where, rows_t, weights, other_x, other_z, 1, own)
    visit_rows = jnp.sum(row_sums[:3], axis=0)
    total_rows = jnp.sum(row_sums[:6], axis=0)
    visit_cols = jnp.sum(col_sums[:3], axis=0)
    total_cols = jnp.sum(col_sums[:6], axis=0)
    for step in range(ITERS):
        ratio_rows = visit_rows / total_rows
        ratio_cols = visit_cols / total_cols
        estimate = sym / (ratio_rows[:, None] + ratio_cols[None, :])
        totals = jnp.sum(to_all(jnp.sum(estimate, axis=1)), axis=1).reshape(STATES)
        total_rows = lax.dynamic_slice_in_dim(totals, w * WIDTH, WIDTH)
        total_cols = lax.dynamic_slice_in_dim(totals, y * COLS, COLS)
    transition = STATES * estimate / total_rows[:, None]
    stationary = STATES * total_rows / jnp.sum(totals)
    return (transition, stationary)


def solution(mesh):
    mesh = Mesh(mesh.devices.reshape(4, 4, 2, 4), ALL)
    return jax.shard_map(
        shards,
        mesh=mesh,
        in_specs=(P("y", WIDE),),
        out_specs=(P(WIDE, "y"), P(WIDE)),
        check_vma=False,
    )
```

```python
import jax
import jax.numpy as jnp
from jax import lax
from jax.experimental import pallas as pl
from jax.experimental.pallas import tpu as pltpu
from jax.sharding import Mesh, PartitionSpec as P

STATES = 8192
TAU = 64
FRAMES = 2048
WIDE = ("x", "z", "c")
ALL = ("x", "z", "c", "y")
BLOCK = 512
WIDTH = 256
COLS = 2048
GROUPS = COLS // WIDTH
FIRST = 256
STACK = 2 * WIDTH + 16
LANES = 128


def place(x, y, z, c):
    return ((x * 4 + z) * 2 + c) * 4 + y


def across():
    return [
        (place(x, y, z, c), place(y, x, z, c))
        for x in range(4) for y in range(4) for z in range(4) for c in range(2)
    ]


def along(k):
    return [(i, (i + k) % 4) for i in range(4)]


def ring(v, axis):
    return [v] + [lax.ppermute(v, axis, along(k)) for k in (1, 2, 3)]


def to_all(sent):
    return lax.all_to_all(sent, ("y",) + WIDE, 0, 0)


VMEM = pl.BlockSpec(memory_space=pltpu.VMEM)
SMEM = pl.BlockSpec(memory_space=pltpu.SMEM)


def f32(*shape):
    return jax.ShapeDtypeStruct(shape, jnp.float32)


def row_parts(sym_ref, ratio_rows, ratio_cols, send_ref):
    parts = []
    for top in range(0, WIDTH, 64):
        acc = jnp.zeros((64, LANES), jnp.float32)
        for k in range(COLS // LANES):
            g, lo = divmod(k * LANES, WIDTH)
            acc += sym_ref[top:top + 64, k * LANES:(k + 1) * LANES] / (
                ratio_rows[top:top + 64] + ratio_cols[g:g + 1, lo:lo + LANES])
        parts.append(acc)
    sums = jnp.sum(jnp.concatenate(parts, axis=0).T, axis=0, keepdims=True)
    send_ref[...] = jnp.broadcast_to(sums, send_ref.shape)


def products(where, left, by_x, by_z, before):
    def kernel(where_ref, left_ref, *refs):
        x_refs, z_refs = refs[:4], refs[4:8]
        x, z, c = where_ref[0], where_ref[2], where_ref[3]
        if before is None:
            sym_ref, visit_ref, total_ref, visit_row_ref, total_row_ref = refs[8:]
            core = c
            sums = lax.dot_general(
                left_ref[:2 * WIDTH], left_ref[2 * WIDTH:], (((1,), (1,)), ((), ())),
                preferred_element_type=jnp.float32)
            sums = jnp.sum(sums[:, 6:9], axis=1, keepdims=True)
            visit = jnp.broadcast_to(sums[:WIDTH], (WIDTH, LANES))
            visit_row_ref[...] = visit
            total_row_ref[...] = visit + sums[WIDTH:]
        else:
            visit_row_ref, total_row_ref = refs[11:13]
            sym_ref, visit_ref, total_ref, send_ref = refs[13:]
            core = 1 - c
            sym_ref[...], visit_ref[...], total_ref[...] = (ref[...] for ref in refs[8:11])
        for dz in range(4):
            acc = jnp.zeros((STACK, WIDTH), jnp.float32)
            for dx in range(4):
                lo = pl.multiple_of(lax.rem(x + 4 - dx, 4) * BLOCK, BLOCK)
                block = jnp.concatenate([x_refs[dx][dz], z_refs[dz][dx]], axis=0)
                acc += jnp.dot(left_ref[:, pl.ds(lo, BLOCK)], block,
                               preferred_element_type=jnp.float32)
            g = lax.rem(z + 4 - dz, 4) * 2 + core
            sym_ref[:, pl.ds(pl.multiple_of(g * WIDTH, WIDTH), WIDTH)] = (
                acc[:WIDTH] + acc[WIDTH:2 * WIDTH])
            frame = acc[2 * WIDTH:]
            visit_ref[pl.ds(g, 1), :] = jnp.sum(frame[:3], axis=0, keepdims=True)
            total_ref[pl.ds(g, 1), :] = jnp.sum(frame[:6], axis=0, keepdims=True)
        if before is not None:
            row_parts(sym_ref, visit_row_ref[...] / total_row_ref[...],
                      visit_ref[...] / total_ref[...], send_ref)

    operands = [where, left] + by_x + by_z
    out = [f32(WIDTH, COLS), f32(GROUPS, WIDTH), f32(GROUPS, WIDTH)]
    if before is None:
        out += [f32(WIDTH, LANES)] * 2
    else:
        operands += list(before)
        out += [f32(128, WIDTH)]
    return pl.pallas_call(
        kernel,
        in_specs=[SMEM] + [VMEM] * (len(operands) - 1),
        out_specs=[VMEM] * len(out),
        out_shape=out,
    )(*operands)


def totals_of(where_ref, got_ref, total_ref):
    total_ref[...] = sum(got_ref[32 * k:32 * k + 32, :] for k in range(4))
    x, y, z, c = (where_ref[i] for i in range(4))
    cols = total_ref[pl.ds(pl.multiple_of(y * GROUPS, GROUPS), GROUPS), :]
    own = total_ref[pl.ds((x * 4 + z) * 2 + c, 1), :]
    return cols, own, jnp.broadcast_to(own, (LANES, WIDTH)).T


def iterate(where, got, sym, visit, visit_row):
    def kernel(where_ref, got_ref, sym_ref, visit_ref, visit_row_ref, send_ref, row_ref, col_ref,
               total_ref):
        cols, _, down = totals_of(where_ref, got_ref, total_ref)
        row_ref[...] = visit_row_ref[...] / down
        col_ref[...] = visit_ref[...] / cols
        row_parts(sym_ref, row_ref[...], col_ref[...], send_ref)

    return pl.pallas_call(
        kernel,
        in_specs=[SMEM] + [VMEM] * 4,
        out_specs=[VMEM] * 3,
        out_shape=[f32(128, WIDTH), f32(WIDTH, LANES), f32(GROUPS, WIDTH)],
        scratch_shapes=[pltpu.VMEM((32, WIDTH), jnp.float32)],
    )(where, got, sym, visit, visit_row)


def finish(where, got, sym, ratio_row, ratio_col):
    def kernel(where_ref, got_ref, sym_ref, row_ref, col_ref, out_ref, share_ref, total_ref, down_ref):
        g = pl.program_id(0)

        @pl.when(g == 0)
        def _():
            _, own, down = totals_of(where_ref, got_ref, total_ref)
            down_ref[...] = STATES / down
            everything = jnp.sum(jnp.sum(total_ref[...], axis=0, keepdims=True), axis=1, keepdims=True)
            share_ref[...] = STATES * own / everything

        col = col_ref[pl.ds(g, 1), :]
        for k in range(WIDTH // LANES):
            lo = k * LANES
            at = pl.multiple_of(g * WIDTH + lo, LANES)
            out_ref[:, lo:lo + LANES] = down_ref[...] * (
                sym_ref[:, pl.ds(at, LANES)] / (row_ref[...] + col[:, lo:lo + LANES]))

    whole = lambda v: pl.BlockSpec(v.shape, lambda g: (0, 0))
    return pl.pallas_call(
        kernel,
        grid=(GROUPS,),
        in_specs=[SMEM, whole(got), whole(sym), whole(ratio_row), whole(ratio_col)],
        out_specs=[pl.BlockSpec((WIDTH, WIDTH), lambda g: (0, g)),
                   pl.BlockSpec((1, WIDTH), lambda g: (0, 0))],
        out_shape=[f32(WIDTH, COLS), f32(1, WIDTH)],
        scratch_shapes=[pltpu.VMEM((32, WIDTH), jnp.float32), pltpu.VMEM((WIDTH, LANES), jnp.float32)],
    )(where, got, sym, ratio_row, ratio_col)


def three_parts(v):
    hi = v.astype(jnp.bfloat16)
    rest = v - hi.astype(jnp.float32)
    mid = rest.astype(jnp.bfloat16)
    lo = (rest - mid.astype(jnp.float32)).astype(jnp.bfloat16)
    return [hi, mid, lo]


def own_rows(member):
    y = lax.axis_index("y")
    later = [lax.ppermute(member, "y", along(-k)) for k in (1, 2, 3)]
    turned = jnp.concatenate([member] + later, axis=0).T
    rows = jnp.roll(turned, y * BLOCK, axis=1)
    return jnp.pad(rows, ((0, 0), (TAU, TAU)))


def frame_weights(member):
    part = jnp.sum(member, axis=1, dtype=jnp.float32)
    got = to_all(jnp.broadcast_to(part[None], (128, BLOCK)))
    frame = jnp.sum(got.reshape(4, 32, BLOCK), axis=1).reshape(FRAMES)
    up = jnp.pad(frame[TAU:], (0, TAU))
    down = jnp.pad(frame[:FRAMES - TAU], (TAU, 0))
    weights = jnp.stack(three_parts(up) + three_parts(down) + three_parts(frame))
    return jnp.pad(weights, ((0, 7), (0, 0)))


def shards(member):
    where = jnp.stack([lax.axis_index(a) for a in ("x", "y", "z", "c")])
    moved = lax.ppermute(member, ALL, across())
    once_x = jnp.stack(ring(moved[:FIRST], "z"))
    once_z = jnp.stack(ring(moved[FIRST:], "x"))
    once_x, once_z, kept = lax.optimization_barrier((once_x, once_z, member))
    by_x = ring(once_x, "x")
    by_z = ring(once_z, "z")
    swap = [(0, 1), (1, 0)]
    other_x = [lax.ppermute(v, "c", swap) for v in by_x]
    other_z = [lax.ppermute(v, "c", swap) for v in by_z]
    rows = own_rows(kept)
    left = jnp.concatenate([rows[:, :FRAMES], rows[:, 2 * TAU:], frame_weights(member)], axis=0)
    own = products(where, left, by_x, by_z, None)
    sym, visit, _, send = products(where, left, other_x, other_z, own)
    visit_row = own[3]
    for step in range(2):
        send, ratio_row, ratio_col = iterate(where, to_all(send), sym, visit, visit_row)
    transition, stationary = finish(where, to_all(send), sym, ratio_row, ratio_col)
    return (transition, stationary.reshape(WIDTH))


def solution(mesh):
    mesh = Mesh(mesh.devices.reshape(4, 4, 2, 4), ALL)
    return jax.shard_map(
        shards,
        mesh=mesh,
        in_specs=(P("y", WIDE),),
        out_specs=(P(WIDE, "y"), P(WIDE)),
        check_vma=False,
    )
```

```python
import jax
import jax.numpy as jnp
from jax import lax
from jax.experimental import pallas as pl
from jax.experimental.pallas import tpu as pltpu
from jax.sharding import Mesh, PartitionSpec as P


STATES = 8192
TAU = 64
FRAMES = 2048
WIDE = ("x", "z", "c")
ALL = ("x", "z", "c", "y")
BLOCK = 512
WIDTH = 256
COLS = 2048
GROUPS = COLS // WIDTH
FIRST = 256
STACK = 2 * WIDTH + 16
LANES = 128


def place(x, y, z, c):
    return ((x * 4 + z) * 2 + c) * 4 + y


def across():
    return [
        (place(x, y, z, c), place(y, x, z, c))
        for x in range(4) for y in range(4) for z in range(4) for c in range(2)
    ]


def along(k):
    return [(i, (i + k) % 4) for i in range(4)]


def ring(v, axis):
    return [v] + [lax.ppermute(v, axis, along(k)) for k in (1, 2, 3)]


def to_all(values):
    sent = jnp.broadcast_to(values[None], (128,) + values.shape)
    return lax.all_to_all(sent, ALL, 0, 0).reshape((32, 4) + values.shape)


VMEM = pl.BlockSpec(memory_space=pltpu.VMEM)
SMEM = pl.BlockSpec(memory_space=pltpu.SMEM)


def f32(*shape):
    return jax.ShapeDtypeStruct(shape, jnp.float32)


def row_parts(sym_ref, ratio_rows, ratio_cols):
    parts = []
    for top in range(0, WIDTH, 64):
        acc = jnp.zeros((64, LANES), jnp.float32)
        for k in range(COLS // LANES):
            g, lo = divmod(k * LANES, WIDTH)
            acc += sym_ref[top:top + 64, k * LANES:(k + 1) * LANES] / (
                ratio_rows[top:top + 64] + ratio_cols[g:g + 1, lo:lo + LANES])
        parts.append(acc)
    return jnp.sum(jnp.concatenate(parts, axis=0).T, axis=0, keepdims=True)


def products(where, left, by_x, by_z, before):
    def kernel(where_ref, left_ref, *refs):
        x_refs, z_refs = refs[:4], refs[4:8]
        x, z, c = where_ref[0], where_ref[2], where_ref[3]
        if before is None:
            sym_ref, visit_ref, total_ref, visit_row_ref, total_row_ref = refs[8:]
            core = c
            sums = lax.dot_general(
                left_ref[:2 * WIDTH], left_ref[2 * WIDTH:], (((1,), (1,)), ((), ())),
                preferred_element_type=jnp.float32)
            sums = jnp.sum(sums[:, 6:9], axis=1, keepdims=True)
            visit = jnp.broadcast_to(sums[:WIDTH], (WIDTH, LANES))
            visit_row_ref[...] = visit
            total_row_ref[...] = visit + sums[WIDTH:]
        else:
            visit_row_ref, total_row_ref = refs[11:13]
            sym_ref, visit_ref, total_ref, send_ref = refs[13:]
            core = 1 - c
            sym_ref[...], visit_ref[...], total_ref[...] = (ref[...] for ref in refs[8:11])
        for dz in range(4):
            acc = jnp.zeros((STACK, WIDTH), jnp.float32)
            for dx in range(4):
                lo = pl.multiple_of(lax.rem(x + 4 - dx, 4) * BLOCK, BLOCK)
                block = jnp.concatenate([x_refs[dx][dz], z_refs[dz][dx]], axis=0)
                acc += jnp.dot(left_ref[:, pl.ds(lo, BLOCK)], block,
                               preferred_element_type=jnp.float32)
            g = lax.rem(z + 4 - dz, 4) * 2 + core
            sym_ref[:, pl.ds(pl.multiple_of(g * WIDTH, WIDTH), WIDTH)] = (
                acc[:WIDTH] + acc[WIDTH:2 * WIDTH])
            frame = acc[2 * WIDTH:]
            visit_ref[pl.ds(g, 1), :] = jnp.sum(frame[:3], axis=0, keepdims=True)
            total_ref[pl.ds(g, 1), :] = jnp.sum(frame[:6], axis=0, keepdims=True)
        if before is not None:
            send_ref[...] = row_parts(sym_ref, visit_row_ref[...] / total_row_ref[...],
                                      visit_ref[...] / total_ref[...])

    operands = [where, left] + by_x + by_z
    out = [f32(WIDTH, COLS), f32(GROUPS, WIDTH), f32(GROUPS, WIDTH)]
    if before is None:
        out += [f32(WIDTH, LANES)] * 2
    else:
        operands += list(before)
        out += [f32(1, WIDTH)]
    return pl.pallas_call(
        kernel,
        in_specs=[SMEM] + [VMEM] * (len(operands) - 1),
        out_specs=[VMEM] * len(out),
        out_shape=out,
        compiler_params=pltpu.CompilerParams(vmem_limit_bytes=16 << 20),
    )(*[operands[0]] + [pltpu.with_memory_space_constraint(v, pltpu.VMEM) for v in operands[1:]])


def three_parts(v):
    hi = v.astype(jnp.bfloat16)
    rest = v - hi.astype(jnp.float32)
    mid = rest.astype(jnp.bfloat16)
    lo = (rest - mid.astype(jnp.float32)).astype(jnp.bfloat16)
    return [hi, mid, lo]


def own_rows(member):
    y = lax.axis_index("y")
    later = [lax.ppermute(member, "y", along(-k)) for k in (1, 2, 3)]
    turned = jnp.concatenate([member] + later, axis=0).T
    rows = jnp.roll(turned, y * BLOCK, axis=1)
    return jnp.pad(rows, ((0, 0), (TAU, TAU)))


def frame_weights(member, after):
    part = jnp.sum(member, axis=1, dtype=jnp.float32)
    got = to_all(part)
    got, _ = lax.optimization_barrier((got, after))
    frame = jnp.sum(got, axis=0).reshape(FRAMES)
    up = jnp.pad(frame[TAU:], (0, TAU))
    down = jnp.pad(frame[:FRAMES - TAU], (TAU, 0))
    weights = jnp.stack(three_parts(up) + three_parts(down) + three_parts(frame))
    return jnp.pad(weights, ((0, 7), (0, 0)))


def shards(member):
    where = jnp.stack([lax.axis_index(a) for a in ("x", "y", "z", "c")])
    moved = lax.ppermute(member, ALL, across())
    once_x = jnp.stack(ring(moved[:FIRST], "z"))
    once_z = jnp.stack(ring(moved[FIRST:], "x"))
    by_x = ring(once_x, "x")
    by_z = ring(once_z, "z")
    other_x = [lax.ppermute(v, "c", [(0, 1), (1, 0)]) for v in by_x]
    other_z = [lax.ppermute(v, "c", [(0, 1), (1, 0)]) for v in by_z]
    rows = own_rows(member)
    left = jnp.concatenate([rows[:, :FRAMES], rows[:, 2 * TAU:], frame_weights(member, (once_x, once_z))], axis=0)
    own = products(where, left, by_x, by_z, None)
    sym, visit_cols, _, part = products(where, left, other_x, other_z, own)
    visit_cols = visit_cols.reshape(COLS)
    visit_rows = own[3][:, 0]
    part = part.reshape(WIDTH)
    w = (where[0] * 4 + where[2]) * 2 + where[3]
    for step in range(3):
        totals = jnp.sum(to_all(part), axis=1).reshape(STATES)
        total_rows = lax.dynamic_slice_in_dim(totals, w * WIDTH, WIDTH)
        total_cols = lax.dynamic_slice_in_dim(totals, where[1] * COLS, COLS)
        if step == 2:
            break
        estimate = sym / ((visit_rows / total_rows)[:, None] + (visit_cols / total_cols)[None, :])
        part = jnp.sum(estimate, axis=1)
    transition = STATES * estimate / total_rows[:, None]
    stationary = STATES * total_rows / jnp.sum(totals)
    return (transition, stationary)


def solution(mesh):
    mesh = Mesh(mesh.devices.reshape(4, 4, 2, 4), ALL)
    return jax.shard_map(
        shards,
        mesh=mesh,
        in_specs=(P("y", WIDE),),
        out_specs=(P(WIDE, "y"), P(WIDE)),
        check_vma=False,
    )
```

```python
import jax
import jax.numpy as jnp
from jax import lax
from jax.experimental import pallas as pl
from jax.experimental.pallas import tpu as pltpu
from jax.sharding import Mesh, PartitionSpec as P


STATES = 8192
TAU = 64
FRAMES = 2048
WIDE = ("x", "z", "c")
ALL = ("x", "z", "c", "y")
BLOCK = 512
WIDTH = 256
COLS = 2048
GROUPS = COLS // WIDTH
FIRST = 224
STACK = 2 * WIDTH + 16
LANES = 128


def place(x, y, z, c):
    return ((x * 4 + z) * 2 + c) * 4 + y


def across():
    return [
        (place(x, y, z, c), place(y, x, z, c))
        for x in range(4) for y in range(4) for z in range(4) for c in range(2)
    ]


def along(k):
    return [(i, (i + k) % 4) for i in range(4)]


def ring(v, axis):
    return [v] + [lax.ppermute(v, axis, along(k)) for k in (1, 2, 3)]


def to_all(values):
    sent = jnp.broadcast_to(values[None], (128,) + values.shape)
    return lax.all_to_all(sent, ALL, 0, 0).reshape((32, 4) + values.shape)


VMEM = pl.BlockSpec(memory_space=pltpu.VMEM)
SMEM = pl.BlockSpec(memory_space=pltpu.SMEM)


def f32(*shape):
    return jax.ShapeDtypeStruct(shape, jnp.float32)


def row_parts(sym_ref, ratio_rows, ratio_cols):
    parts = []
    for top in range(0, WIDTH, 64):
        acc = jnp.zeros((64, LANES), jnp.float32)
        for k in range(COLS // LANES):
            g, lo = divmod(k * LANES, WIDTH)
            acc += sym_ref[top:top + 64, k * LANES:(k + 1) * LANES] / (
                ratio_rows[top:top + 64] + ratio_cols[g:g + 1, lo:lo + LANES])
        parts.append(acc)
    return jnp.sum(jnp.concatenate(parts, axis=0).T, axis=0, keepdims=True)


def products(where, left, by_x, by_z, before):
    def kernel(where_ref, left_ref, *refs):
        x_refs, z_refs = refs[:4], refs[4:8]
        x, y, z, c = (where_ref[i] for i in range(4))
        if before is None:
            sym_ref, visit_ref, total_ref, visit_row_ref, total_row_ref = refs[8:]
            core = c
            sums = lax.dot_general(
                left_ref[:2 * WIDTH], left_ref[2 * WIDTH:], (((1,), (1,)), ((), ())),
                preferred_element_type=jnp.float32)
            sums = jnp.sum(sums[:, 6:9], axis=1, keepdims=True)
            visit = jnp.broadcast_to(sums[:WIDTH], (WIDTH, LANES))
            visit_row_ref[...] = visit
            total_row_ref[...] = visit + sums[WIDTH:]
        else:
            visit_row_ref, total_row_ref = refs[11:13]
            sym_ref, visit_ref, total_ref, send_ref = refs[13:]
            core = 1 - c
            sym_ref[...], visit_ref[...], total_ref[...] = (ref[...] for ref in refs[8:11])
        for dz in range(4):
            acc = jnp.zeros((STACK, WIDTH), jnp.float32)
            for dx in range(4):
                lo = pl.multiple_of(lax.rem(x + 4 - dx, 4) * BLOCK, BLOCK)
                rest = z_refs[dz][lax.rem(y + 4 - x + dx, 4)]
                block = jnp.concatenate([x_refs[dx][dz], rest], axis=0)
                acc += jnp.dot(left_ref[:, pl.ds(lo, BLOCK)], block,
                               preferred_element_type=jnp.float32)
            g = lax.rem(z + 4 - dz, 4) * 2 + core
            sym_ref[:, pl.ds(pl.multiple_of(g * WIDTH, WIDTH), WIDTH)] = (
                acc[:WIDTH] + acc[WIDTH:2 * WIDTH])
            frame = acc[2 * WIDTH:]
            visit_ref[pl.ds(g, 1), :] = jnp.sum(frame[:3], axis=0, keepdims=True)
            total_ref[pl.ds(g, 1), :] = jnp.sum(frame[:6], axis=0, keepdims=True)
        if before is not None:
            send_ref[...] = row_parts(sym_ref, visit_row_ref[...] / total_row_ref[...],
                                      visit_ref[...] / total_ref[...])

    operands = [where, left] + by_x + by_z
    out = [f32(WIDTH, COLS), f32(GROUPS, WIDTH), f32(GROUPS, WIDTH)]
    if before is None:
        out += [f32(WIDTH, LANES)] * 2
    else:
        operands += list(before)
        out += [f32(1, WIDTH)]
    return pl.pallas_call(
        kernel,
        in_specs=[SMEM] + [VMEM] * (len(operands) - 1),
        out_specs=[VMEM] * len(out),
        out_shape=out,
        compiler_params=pltpu.CompilerParams(vmem_limit_bytes=16 << 20),
    )(*[operands[0]] + [pltpu.with_memory_space_constraint(v, pltpu.VMEM) for v in operands[1:]])


def three_parts(v):
    hi = v.astype(jnp.bfloat16)
    rest = v - hi.astype(jnp.float32)
    mid = rest.astype(jnp.bfloat16)
    lo = (rest - mid.astype(jnp.float32)).astype(jnp.bfloat16)
    return [hi, mid, lo]


def own_rows(member):
    y = lax.axis_index("y")
    later = [lax.ppermute(member, "y", along(-k)) for k in (1, 2, 3)]
    turned = jnp.concatenate([member] + later, axis=0).T
    rows = jnp.roll(turned, y * BLOCK, axis=1)
    return jnp.pad(rows, ((0, 0), (TAU, TAU)))


def frame_weights(member, after):
    part = jnp.sum(member, axis=1, dtype=jnp.float32)
    got = to_all(part)
    got, _ = lax.optimization_barrier((got, after))
    frame = jnp.sum(got, axis=0).reshape(FRAMES)
    up = jnp.pad(frame[TAU:], (0, TAU))
    down = jnp.pad(frame[:FRAMES - TAU], (TAU, 0))
    weights = jnp.stack(three_parts(up) + three_parts(down) + three_parts(frame))
    return jnp.pad(weights, ((0, 7), (0, 0)))


def shards(member):
    where = jnp.stack([lax.axis_index(a) for a in ("x", "y", "z", "c")])
    x, y = where[0], where[1]
    moved = lax.ppermute(member[:FIRST], ALL, across())
    planes = jnp.stack(ring(member[FIRST:], "x"))
    once_x = jnp.stack(ring(moved, "z"))
    leave = [lax.dynamic_index_in_dim(planes, lax.rem(x + 8 - y - k, 4), 0, False) for k in range(4)]
    once_z = jnp.stack([leave[0]] + [lax.ppermute(leave[k], "y", along(k)) for k in (1, 2, 3)])
    by_x = ring(once_x, "x")
    by_z = ring(once_z, "z")
    other_x = [lax.ppermute(v, "c", [(0, 1), (1, 0)]) for v in by_x]
    other_z = [lax.ppermute(v, "c", [(0, 1), (1, 0)]) for v in by_z]
    rows = own_rows(member)
    left = jnp.concatenate([rows[:, :FRAMES], rows[:, 2 * TAU:], frame_weights(member, (once_x, once_z))], axis=0)
    own = products(where, left, by_x, by_z, None)
    sym, visit_cols, _, part = products(where, left, other_x, other_z, own)
    visit_cols = visit_cols.reshape(COLS)
    visit_rows = own[3][:, 0]
    part = part.reshape(WIDTH)
    w = (where[0] * 4 + where[2]) * 2 + where[3]
    for step in range(3):
        totals = jnp.sum(to_all(part), axis=1).reshape(STATES)
        total_rows = lax.dynamic_slice_in_dim(totals, w * WIDTH, WIDTH)
        total_cols = lax.dynamic_slice_in_dim(totals, where[1] * COLS, COLS)
        if step == 2:
            break
        ratio = (visit_rows / total_rows)[:, None] + (visit_cols / total_cols)[None, :]
        part = jnp.sum(sym / ratio, axis=1)
    transition = sym * (STATES / total_rows)[:, None] / ratio
    stationary = STATES * total_rows / jnp.sum(totals)
    return (transition, stationary)


def solution(mesh):
    mesh = Mesh(mesh.devices.reshape(4, 4, 2, 4), ALL)
    return jax.shard_map(
        shards,
        mesh=mesh,
        in_specs=(P("y", WIDE),),
        out_specs=(P(WIDE, "y"), P(WIDE)),
        check_vma=False,
    )
```

```python
import jax
import jax.numpy as jnp
from jax import lax
from jax.experimental import pallas as pl
from jax.experimental.pallas import tpu as pltpu
from jax.sharding import Mesh, PartitionSpec as P


STATES = 8192
TAU = 64
FRAMES = 2048
WIDE = ("x", "z", "c")
ALL = ("x", "z", "c", "y")
BLOCK = 512
WIDTH = 256
COLS = 2048
GROUPS = COLS // WIDTH
FIRST = 288
STACK = 2 * WIDTH + 16
LANES = 128


def place(x, y, z, c):
    return ((x * 4 + z) * 2 + c) * 4 + y


def across():
    return [
        (place(x, y, z, c), place(y, x, z, c))
        for x in range(4) for y in range(4) for z in range(4) for c in range(2)
    ]


def along(k):
    return [(i, (i + k) % 4) for i in range(4)]


def ring(v, axis):
    return [v] + [lax.ppermute(v, axis, along(k)) for k in (1, 2, 3)]


def to_all(values):
    sent = jnp.broadcast_to(values[None], (128,) + values.shape)
    return lax.all_to_all(sent, ALL, 0, 0).reshape((32, 4) + values.shape)


VMEM = pl.BlockSpec(memory_space=pltpu.VMEM)
SMEM = pl.BlockSpec(memory_space=pltpu.SMEM)


def f32(*shape):
    return jax.ShapeDtypeStruct(shape, jnp.float32)


def row_parts(sym_ref, ratio_rows, ratio_cols):
    parts = []
    for top in range(0, WIDTH, 64):
        acc = jnp.zeros((64, LANES), jnp.float32)
        for k in range(COLS // LANES):
            g, lo = divmod(k * LANES, WIDTH)
            acc += sym_ref[top:top + 64, k * LANES:(k + 1) * LANES] / (
                ratio_rows[top:top + 64] + ratio_cols[g:g + 1, lo:lo + LANES])
        parts.append(acc)
    return jnp.sum(jnp.concatenate(parts, axis=0).T, axis=0, keepdims=True)


def products(where, left, by_x, by_z, before):
    def kernel(where_ref, left_ref, *refs):
        x_refs, z_refs = refs[:4], refs[4:8]
        x, y, z, c = (where_ref[i] for i in range(4))
        if before is None:
            sym_ref, visit_ref, total_ref, ratio_ref, visit_row_ref = refs[8:]
            core = c
            sums = lax.dot_general(
                left_ref[:2 * WIDTH], left_ref[2 * WIDTH:], (((1,), (1,)), ((), ())),
                preferred_element_type=jnp.float32)
            sums = jnp.sum(sums[:, 6:9], axis=1, keepdims=True)
            visit = jnp.broadcast_to(sums[:WIDTH], (WIDTH, LANES))
            ratio_ref[...] = visit / (visit + sums[WIDTH:])
            visit_row_ref[...] = visit.T[:1]
        else:
            sym_ref, visit_ref, total_ref, send_ref = refs[12:]
            core = 1 - c
            sym_ref[...], visit_ref[...], total_ref[...] = (ref[...] for ref in refs[8:11])
        for dz in range(4):
            acc = jnp.zeros((STACK, WIDTH), jnp.float32)
            for dx in range(4):
                lo = pl.multiple_of(lax.rem(x + 4 - dx, 4) * BLOCK, BLOCK)
                rest = z_refs[dz][lax.rem(y + 4 - x + dx, 4)]
                block = jnp.concatenate([x_refs[dx][dz], rest], axis=0)
                acc += jnp.dot(left_ref[:, pl.ds(lo, BLOCK)], block,
                               preferred_element_type=jnp.float32)
            g = lax.rem(z + 4 - dz, 4) * 2 + core
            sym_ref[:, pl.ds(pl.multiple_of(g * WIDTH, WIDTH), WIDTH)] = (
                acc[:WIDTH] + acc[WIDTH:2 * WIDTH])
            frame = acc[2 * WIDTH:]
            visit_ref[pl.ds(g, 1), :] = jnp.sum(frame[:3], axis=0, keepdims=True)
            total_ref[pl.ds(g, 1), :] = jnp.sum(frame[:6], axis=0, keepdims=True)
        if before is not None:
            send_ref[...] = row_parts(sym_ref, refs[11][...], visit_ref[...] / total_ref[...])

    operands = [where, left] + by_x + by_z
    out = [f32(WIDTH, COLS), f32(GROUPS, WIDTH), f32(GROUPS, WIDTH)]
    if before is None:
        out += [f32(WIDTH, LANES), f32(1, WIDTH)]
    else:
        operands += list(before[:4])
        out += [f32(1, WIDTH)]
    return pl.pallas_call(
        kernel,
        in_specs=[SMEM] + [VMEM] * (len(operands) - 1),
        out_specs=[VMEM] * len(out),
        out_shape=out,
        compiler_params=pltpu.CompilerParams(vmem_limit_bytes=16 << 20),
    )(*[operands[0]] + [pltpu.with_memory_space_constraint(v, pltpu.VMEM) for v in operands[1:]])


def three_parts(v):
    hi = v.astype(jnp.bfloat16)
    rest = v - hi.astype(jnp.float32)
    mid = rest.astype(jnp.bfloat16)
    lo = (rest - mid.astype(jnp.float32)).astype(jnp.bfloat16)
    return [hi, mid, lo]


def own_rows(member):
    y = lax.axis_index("y")
    later = [lax.ppermute(member, "y", along(-k)) for k in (1, 2, 3)]
    turned = jnp.concatenate([member] + later, axis=0).T
    rows = jnp.roll(turned, y * BLOCK, axis=1)
    return jnp.pad(rows, ((0, 0), (TAU, TAU)))


def frame_weights(member):
    part = jnp.sum(member, axis=1, dtype=jnp.float32)
    got = to_all(part)
    frame = jnp.sum(got, axis=0).reshape(FRAMES)
    up = jnp.pad(frame[TAU:], (0, TAU))
    down = jnp.pad(frame[:FRAMES - TAU], (TAU, 0))
    weights = jnp.stack(three_parts(up) + three_parts(down) + three_parts(frame))
    return jnp.pad(weights, ((0, 7), (0, 0)))


def shards(member):
    where = jnp.stack([lax.axis_index(a) for a in ("x", "y", "z", "c")])
    x, y = where[0], where[1]
    moved = lax.ppermute(member[:FIRST], ALL, across())
    planes = jnp.stack(ring(member[FIRST:], "x"))
    once_x = jnp.stack(ring(moved, "z"))
    leave = [lax.dynamic_index_in_dim(planes, lax.rem(x + 8 - y - k, 4), 0, False) for k in range(4)]
    once_z = jnp.stack([leave[0]] + [lax.ppermute(leave[k], "y", along(k)) for k in (1, 2, 3)])
    by_x = ring(once_x, "x")
    by_z = ring(once_z, "z")
    other_x = [lax.ppermute(v, "c", [(0, 1), (1, 0)]) for v in by_x]
    other_z = [lax.ppermute(v, "c", [(0, 1), (1, 0)]) for v in by_z]
    rows = own_rows(member)
    left = jnp.concatenate([rows[:, :FRAMES], rows[:, 2 * TAU:], frame_weights(member)], axis=0)
    own = products(where, left, by_x, by_z, None)
    sym, visit_cols, _, part = products(where, left, other_x, other_z, own)
    w = (x * 4 + where[2]) * 2 + where[3]
    for step in range(3):
        totals = jnp.sum(to_all(part.reshape(WIDTH)), axis=1)
        total_rows = lax.dynamic_slice_in_dim(totals, w, 1).reshape(WIDTH)
        total_cols = lax.dynamic_slice_in_dim(totals, y * GROUPS, GROUPS)
        if step == 2:
            break
        ratio_rows = own[4].reshape(WIDTH) / total_rows
        ratio = ratio_rows[:, None] + (visit_cols / total_cols).reshape(COLS)[None, :]
        part = jnp.sum(sym / ratio, axis=1)
    transition = sym * (STATES / total_rows)[:, None] / ratio
    stationary = STATES * total_rows / jnp.sum(totals)
    return (transition, stationary)


def solution(mesh):
    mesh = Mesh(mesh.devices.reshape(4, 4, 2, 4), ALL)
    return jax.shard_map(
        shards,
        mesh=mesh,
        in_specs=(P("y", WIDE),),
        out_specs=(P(WIDE, "y"), P(WIDE)),
        check_vma=False,
    )
```

```python
import jax
import jax.numpy as jnp
from jax import lax
from jax.experimental import pallas as pl
from jax.experimental.pallas import tpu as pltpu
from jax.sharding import Mesh, PartitionSpec as P


STATES = 8192
TAU = 64
FRAMES = 2048
WIDE = ("x", "z", "c")
ALL = ("x", "z", "c", "y")
BLOCK = 512
WIDTH = 256
COLS = 2048
GROUPS = COLS // WIDTH
FIRST = 256
STACK = WIDTH + 16
LANES = 128


def place(x, y, z, c):
    return ((x * 4 + z) * 2 + c) * 4 + y


def across():
    return [
        (place(x, y, z, c), place(y, x, z, c))
        for x in range(4) for y in range(4) for z in range(4) for c in range(2)
    ]


def along(k):
    return [(i, (i + k) % 4) for i in range(4)]


def ring(v, axis):
    return [v] + [lax.ppermute(v, axis, along(k)) for k in (1, 2, 3)]


def to_all(values):
    sent = jnp.broadcast_to(values[None], (128,) + values.shape)
    return lax.all_to_all(sent, ALL, 0, 0).reshape((32, 4) + values.shape)


VMEM = pl.BlockSpec(memory_space=pltpu.VMEM)
SMEM = pl.BlockSpec(memory_space=pltpu.SMEM)


def f32(*shape):
    return jax.ShapeDtypeStruct(shape, jnp.float32)


def row_parts(sym_ref, ratio_rows, ratio_cols):
    parts = []
    for top in range(0, WIDTH, 64):
        acc = jnp.zeros((64, LANES), jnp.float32)
        for k in range(COLS // LANES):
            g, lo = divmod(k * LANES, WIDTH)
            acc += sym_ref[top:top + 64, k * LANES:(k + 1) * LANES] / (
                ratio_rows[top:top + 64] + ratio_cols[g:g + 1, lo:lo + LANES])
        parts.append(acc)
    return jnp.sum(jnp.concatenate(parts, axis=0).T, axis=0, keepdims=True)


def products(where, left, by_x, by_z, before):
    def kernel(where_ref, left_ref, *refs):
        x_refs, z_refs = refs[:4], refs[4:8]
        x, _, z, c = (where_ref[i] for i in range(4))
        if before is None:
            sym_ref, visit_ref, total_ref = refs[8:]
            core = c
        else:
            sym_ref, visit_ref, total_ref, send_ref = refs[12:]
            core = 1 - c
            sym_ref[...], visit_ref[...], total_ref[...] = (ref[...] for ref in refs[8:11])
        for dz in range(4):
            acc = jnp.zeros((STACK, WIDTH), jnp.float32)
            for dx in range(4):
                lo = pl.multiple_of(lax.rem(x + 4 - dx, 4) * BLOCK, BLOCK)
                block = jnp.concatenate([x_refs[dx][dz], z_refs[dz][dx]], axis=0)
                acc += jnp.dot(left_ref[:, pl.ds(lo, BLOCK)], block,
                               preferred_element_type=jnp.float32)
            g = lax.rem(z + 4 - dz, 4) * 2 + core
            sym_ref[:, pl.ds(pl.multiple_of(g * WIDTH, WIDTH), WIDTH)] = acc[:WIDTH]
            frame = acc[WIDTH:]
            visit_ref[pl.ds(g, 1), :] = jnp.sum(frame[:3], axis=0, keepdims=True)
            total_ref[pl.ds(g, 1), :] = jnp.sum(frame[:6], axis=0, keepdims=True)
        if before is not None:
            send_ref[...] = row_parts(sym_ref, refs[11][...], visit_ref[...] / total_ref[...])

    operands = [where, left] + by_x + by_z
    out = [f32(WIDTH, COLS), f32(GROUPS, WIDTH), f32(GROUPS, WIDTH)]
    if before is not None:
        operands += list(before)
        out += [f32(1, WIDTH)]
    return pl.pallas_call(
        kernel,
        in_specs=[SMEM] + [VMEM] * (len(operands) - 1),
        out_specs=[VMEM] * len(out),
        out_shape=out,
        compiler_params=pltpu.CompilerParams(vmem_limit_bytes=16 << 20),
    )(*[operands[0]] + [pltpu.with_memory_space_constraint(v, pltpu.VMEM) for v in operands[1:]])


def three_parts(v):
    hi = v.astype(jnp.bfloat16).astype(jnp.float32)
    mid = (v - hi).astype(jnp.bfloat16).astype(jnp.float32)
    return [hi, mid, v - hi - mid]


def prepare(where, blocks, frame):
    def kernel(where_ref, *refs):
        frame_ref, left_ref, visit_ref, ratio_ref, rows_ref = refs[4:]
        edge = jnp.zeros((TAU, WIDTH), jnp.bfloat16)
        rows_ref[:TAU, :] = edge
        rows_ref[TAU + FRAMES:, :] = edge
        for k in range(4):
            lo = lax.rem(where_ref[1] + k, 4) * BLOCK + TAU
            rows_ref[pl.ds(pl.multiple_of(lo, TAU), BLOCK), :] = refs[k][...]
        for lo in range(0, FRAMES, 256):
            both = (rows_ref[lo:lo + 256, :].astype(jnp.float32)
                    + rows_ref[lo + 2 * TAU:lo + 2 * TAU + 256, :].astype(jnp.float32))
            left_ref[:WIDTH, lo:lo + 256] = both.T.astype(jnp.bfloat16)
        total = jnp.concatenate([frame_ref[q:q + 1, :] for q in range(4)], axis=1)
        total = jnp.broadcast_to(total, (16, FRAMES))
        at = lax.broadcasted_iota(jnp.int32, (16, FRAMES), 1)
        line = lax.broadcasted_iota(jnp.int32, (16, FRAMES), 0)
        up = jnp.where(at < FRAMES - TAU, pltpu.roll(total, FRAMES - TAU, 1), 0.0)
        down = jnp.where(at >= TAU, pltpu.roll(total, TAU, 1), 0.0)
        weight = jnp.zeros((16, FRAMES), jnp.float32)
        for i, v in enumerate(three_parts(up) + three_parts(down)):
            weight = jnp.where(line == i, v, weight)
        left_ref[WIDTH:, :] = weight.astype(jnp.bfloat16)
        weight = jnp.zeros((16, FRAMES), jnp.float32)
        for i, v in enumerate(three_parts(total)):
            weight = jnp.where(line == i, v, weight)
        weight = weight.astype(jnp.bfloat16)
        visit = jnp.sum(jnp.dot(weight, rows_ref[:FRAMES, :], preferred_element_type=jnp.float32),
                        axis=0, keepdims=True)
        back = jnp.sum(jnp.dot(weight, rows_ref[2 * TAU:, :], preferred_element_type=jnp.float32),
                       axis=0, keepdims=True)
        visit_ref[...] = visit
        ratio_ref[...] = jnp.broadcast_to(visit / (visit + back), (LANES, WIDTH)).T

    return pl.pallas_call(
        kernel,
        in_specs=[SMEM] + [VMEM] * 5,
        out_specs=[VMEM] * 3,
        out_shape=[jax.ShapeDtypeStruct((STACK, FRAMES), jnp.bfloat16), f32(1, WIDTH), f32(WIDTH, LANES)],
        scratch_shapes=[pltpu.VMEM((FRAMES + 2 * TAU, WIDTH), jnp.bfloat16)],
        compiler_params=pltpu.CompilerParams(vmem_limit_bytes=16 << 20),
    )(where, *[pltpu.with_memory_space_constraint(v, pltpu.VMEM) for v in blocks + [frame]])


def shards(member):
    where = jnp.stack([lax.axis_index(a) for a in ("x", "y", "z", "c")])
    x, y, z, c = (where[i] for i in range(4))
    moved = lax.ppermute(member, ALL, across())
    got = to_all(jnp.sum(member, axis=1, dtype=jnp.float32))
    once_x = jnp.stack(ring(moved[:FIRST], "z"))
    once_z = jnp.stack(ring(moved[FIRST:], "x"))
    got, _ = lax.optimization_barrier((got, (once_x, once_z)))
    by_x = ring(once_x, "x")
    by_z = ring(once_z, "z")
    blocks = [member] + [lax.ppermute(member, "y", along(-k)) for k in (1, 2, 3)]
    other_x = [lax.ppermute(v, "c", [(0, 1), (1, 0)]) for v in by_x]
    other_z = [lax.ppermute(v, "c", [(0, 1), (1, 0)]) for v in by_z]
    left, visit_rows, ratio_rows = prepare(where, blocks, jnp.sum(got, axis=0))
    own = products(where, left, by_x, by_z, None)
    sym, visit_cols, _, part = products(where, left, other_x, other_z, list(own) + [ratio_rows])
    w = (x * 4 + z) * 2 + c
    for step in range(3):
        totals = jnp.sum(to_all(part.reshape(WIDTH)), axis=1)
        total_rows = lax.dynamic_slice_in_dim(totals, w, 1).reshape(WIDTH)
        total_cols = lax.dynamic_slice_in_dim(totals, y * GROUPS, GROUPS)
        if step == 2:
            break
        ratio_rows = visit_rows.reshape(WIDTH) / total_rows
        ratio = ratio_rows[:, None] + (visit_cols / total_cols).reshape(COLS)[None, :]
        part = jnp.sum(sym / ratio, axis=1)
    transition = sym * (STATES / total_rows)[:, None] / ratio
    stationary = STATES * total_rows / jnp.sum(totals)
    return (transition, stationary)


def solution(mesh):
    mesh = Mesh(mesh.devices.reshape(4, 4, 2, 4), ALL)
    return jax.shard_map(
        shards,
        mesh=mesh,
        in_specs=(P("y", WIDE),),
        out_specs=(P(WIDE, "y"), P(WIDE)),
        check_vma=False,
    )
```

```python
import jax
import jax.numpy as jnp
from jax import lax
from jax.experimental import pallas as pl
from jax.experimental.pallas import tpu as pltpu
from jax.sharding import Mesh, PartitionSpec as P


STATES = 8192
TAU = 64
FRAMES = 2048
WIDE = ("x", "z", "c")
ALL = ("x", "z", "c", "y")
BLOCK = 512
WIDTH = 256
COLS = 2048
GROUPS = COLS // WIDTH
FIRST = 256
STACK = 2 * WIDTH + 16
PART = WIDTH + 16
LANES = 128


def place(x, y, z, c):
    return ((x * 4 + z) * 2 + c) * 4 + y


def across():
    return [
        (place(x, y, z, c), place(y, x, z, c))
        for x in range(4) for y in range(4) for z in range(4) for c in range(2)
    ]


def along(k):
    return [(i, (i + k) % 4) for i in range(4)]


def ring(v, axis):
    return [v] + [lax.ppermute(v, axis, along(k)) for k in (1, 2, 3)]


def to_all(values):
    sent = jnp.broadcast_to(values[None], (128,) + values.shape)
    return lax.all_to_all(sent, ALL, 0, 0).reshape((32, 4) + values.shape)


VMEM = pl.BlockSpec(memory_space=pltpu.VMEM)
SMEM = pl.BlockSpec(memory_space=pltpu.SMEM)


def f32(*shape):
    return jax.ShapeDtypeStruct(shape, jnp.float32)


def row_parts(sym_ref, ratio_rows, ratio_cols):
    parts = []
    for top in range(0, WIDTH, 64):
        acc = jnp.zeros((64, LANES), jnp.float32)
        for k in range(COLS // LANES):
            g, lo = divmod(k * LANES, WIDTH)
            acc += sym_ref[top:top + 64, k * LANES:(k + 1) * LANES] / (
                ratio_rows[top:top + 64] + ratio_cols[g:g + 1, lo:lo + LANES])
        parts.append(acc)
    return jnp.sum(jnp.concatenate(parts, axis=0).T, axis=0, keepdims=True)


def grouped(acc):
    return jnp.concatenate([acc[:WIDTH] + acc[WIDTH:2 * WIDTH], acc[2 * WIDTH:]], axis=0)


def call(kernel, out, *operands):
    return pl.pallas_call(
        kernel,
        in_specs=[SMEM] + [VMEM] * (len(operands) - 1),
        out_specs=[VMEM] * len(out),
        out_shape=out,
        compiler_params=pltpu.CompilerParams(vmem_limit_bytes=16 << 20),
    )(operands[0], *[pltpu.with_memory_space_constraint(v, pltpu.VMEM) for v in operands[1:]])


def left_of(where_ref, left_ref, dx, late):
    lo = lax.rem(where_ref[0] + 4 - dx, 4) * BLOCK + late * FIRST
    return left_ref[:, pl.ds(pl.multiple_of(lo, FIRST), FIRST)]


NEAR = (0, 1, 3)


def near(where, left, by_x, by_z):
    def kernel(where_ref, left_ref, *refs):
        x_refs, z_refs, out_ref = refs[:3], refs[3:6], refs[6]
        for dz in range(4):
            acc = jnp.zeros((STACK, WIDTH), jnp.float32)
            for i, dx in enumerate(NEAR):
                acc += jnp.dot(left_of(where_ref, left_ref, dx, 0), x_refs[i][dz],
                               preferred_element_type=jnp.float32)
            if dz in NEAR:
                for dx in range(4):
                    acc += jnp.dot(left_of(where_ref, left_ref, dx, 1), z_refs[NEAR.index(dz)][dx],
                                   preferred_element_type=jnp.float32)
            out_ref[dz] = grouped(acc)

    return call(kernel, [f32(4, PART, WIDTH)], where, left, *by_x, *by_z)[0]


def far_sums(where_ref, left_ref, x_refs, z_refs, dz):
    acc = jnp.dot(left_of(where_ref, left_ref, 2, 0), x_refs[dz // 2][dz % 2],
                  preferred_element_type=jnp.float32)
    if dz == 2:
        for dx in range(4):
            acc += jnp.dot(left_of(where_ref, left_ref, dx, 1), z_refs[dx // 2][dx % 2],
                           preferred_element_type=jnp.float32)
    return grouped(acc)


def far(where, left, by_x, by_z, so_far):
    def kernel(where_ref, left_ref, xa, xb, za, zb, near_ref, out_ref):
        for dz in range(4):
            out_ref[dz] = near_ref[dz] + far_sums(where_ref, left_ref, (xa, xb), (za, zb), dz)

    return call(kernel, [f32(4, PART, WIDTH)], where, left, *by_x, *by_z, so_far)[0]


def far_and_first(where, left, by_x, by_z, so_far, own, ratio_rows):
    def kernel(where_ref, left_ref, xa, xb, za, zb, near_ref, own_ref, ratio_ref,
               sym_ref, visit_ref, send_ref, total_ref):
        z, c = where_ref[2], where_ref[3]
        for dz in range(4):
            mine = own_ref[dz]
            theirs = near_ref[dz] + far_sums(where_ref, left_ref, (xa, xb), (za, zb), dz)
            for core, part in ((c, mine), (1 - c, theirs)):
                g = lax.rem(z + 4 - dz, 4) * 2 + core
                sym_ref[:, pl.ds(pl.multiple_of(g * WIDTH, WIDTH), WIDTH)] = part[:WIDTH]
                frame = part[WIDTH:]
                visit_ref[pl.ds(g, 1), :] = jnp.sum(frame[:3], axis=0, keepdims=True)
                total_ref[pl.ds(g, 1), :] = jnp.sum(frame[:6], axis=0, keepdims=True)
        send_ref[...] = row_parts(sym_ref, ratio_ref[...], visit_ref[...] / total_ref[...])

    out = [f32(WIDTH, COLS), f32(GROUPS, WIDTH), f32(1, WIDTH), f32(GROUPS, WIDTH)]
    return call(kernel, out, where, left, *by_x, *by_z, so_far, own, ratio_rows)[:3]


def three_parts(v):
    hi = v.astype(jnp.bfloat16).astype(jnp.float32)
    mid = (v - hi).astype(jnp.bfloat16).astype(jnp.float32)
    return [hi, mid, v - hi - mid]


def prepare(where, blocks, frames):
    def kernel(where_ref, *refs):
        frame_ref, left_ref, visit_ref, ratio_ref, rows_ref = refs[4:]
        edge = jnp.zeros((TAU, WIDTH), jnp.bfloat16)
        rows_ref[:TAU, :] = edge
        rows_ref[TAU + FRAMES:, :] = edge
        for k in range(4):
            lo = lax.rem(where_ref[1] + k, 4) * BLOCK + TAU
            rows_ref[pl.ds(pl.multiple_of(lo, TAU), BLOCK), :] = refs[k][...]
        for lo in range(0, FRAMES + 2 * TAU, LANES):
            turned = rows_ref[lo:lo + LANES, :].astype(jnp.float32).T.astype(jnp.bfloat16)
            if lo < FRAMES:
                left_ref[:WIDTH, lo:lo + LANES] = turned
            if lo >= 2 * TAU:
                left_ref[WIDTH:2 * WIDTH, lo - 2 * TAU:lo - 2 * TAU + LANES] = turned
        total = jnp.concatenate(
            [jnp.sum(frame_ref[32 * q:32 * q + 32, :], axis=0, keepdims=True) for q in range(4)], axis=1)
        total = jnp.broadcast_to(total, (16, FRAMES))
        at = lax.broadcasted_iota(jnp.int32, (16, FRAMES), 1)
        line = lax.broadcasted_iota(jnp.int32, (16, FRAMES), 0)
        up = jnp.where(at < FRAMES - TAU, pltpu.roll(total, FRAMES - TAU, 1), 0.0)
        down = jnp.where(at >= TAU, pltpu.roll(total, TAU, 1), 0.0)
        weight = jnp.zeros((16, FRAMES), jnp.float32)
        for i, v in enumerate(three_parts(up) + three_parts(down)):
            weight = jnp.where(line == i, v, weight)
        left_ref[2 * WIDTH:, :] = weight.astype(jnp.bfloat16)
        weight = jnp.zeros((16, FRAMES), jnp.float32)
        for i, v in enumerate(three_parts(total)):
            weight = jnp.where(line == i, v, weight)
        weight = weight.astype(jnp.bfloat16)
        visit = jnp.sum(jnp.dot(weight, rows_ref[:FRAMES, :], preferred_element_type=jnp.float32),
                        axis=0, keepdims=True)
        back = jnp.sum(jnp.dot(weight, rows_ref[2 * TAU:, :], preferred_element_type=jnp.float32),
                       axis=0, keepdims=True)
        visit_ref[...] = visit
        ratio_ref[...] = jnp.broadcast_to(visit / (visit + back), (LANES, WIDTH)).T

    return pl.pallas_call(
        kernel,
        in_specs=[SMEM] + [VMEM] * 5,
        out_specs=[VMEM] * 3,
        out_shape=[jax.ShapeDtypeStruct((STACK, FRAMES), jnp.bfloat16), f32(1, WIDTH), f32(WIDTH, LANES)],
        scratch_shapes=[pltpu.VMEM((FRAMES + 2 * TAU, WIDTH), jnp.bfloat16)],
        compiler_params=pltpu.CompilerParams(vmem_limit_bytes=16 << 20),
    )(where, *[pltpu.with_memory_space_constraint(v, pltpu.VMEM) for v in blocks + [frames]])


def from_sides(v, axis):
    return [lax.ppermute(v, axis, along(k)) for k in (1, 3)]


def from_afar(sides, axis):
    return [lax.ppermute(sides[0][:2], axis, along(1)), lax.ppermute(sides[1][2:], axis, along(3))]


def swapped(vs):
    return [lax.ppermute(v, "c", [(0, 1), (1, 0)]) for v in vs]


def shards(member):
    where = jnp.stack([lax.axis_index(a) for a in ("x", "y", "z", "c")])
    x, y, z, c = (where[i] for i in range(4))
    moved = lax.ppermute(member, ALL, across())
    part = jnp.sum(member, axis=1, dtype=jnp.float32)
    frames = lax.all_to_all(jnp.broadcast_to(part[None], (128, BLOCK)), ("y",) + WIDE, 0, 0)
    once_x = jnp.stack(ring(moved[:FIRST], "z"))
    once_z = jnp.stack(ring(moved[FIRST:], "x"))
    near_x = from_sides(once_x, "x")
    near_z = from_sides(once_z, "z")
    far_x = from_afar(near_x, "x")
    far_z = from_afar(near_z, "z")
    kept, frames = lax.optimization_barrier((member, frames))
    blocks = [member] + [lax.ppermute(kept, "y", along(-k)) for k in (1, 2, 3)]
    left, visit_rows, ratio_rows = prepare(where, blocks, frames)
    own = near(where, left, [once_x] + near_x, [once_z] + near_z)
    once_x, once_z = swapped([once_x, once_z])
    near_x, near_z = swapped(near_x), swapped(near_z)
    sibling = near(where, left, [once_x] + near_x, [once_z] + near_z)
    own = far(where, left, far_x, far_z, own)
    far_x, far_z = swapped(far_x), swapped(far_z)
    sym, visit_cols, part = far_and_first(where, left, far_x, far_z, sibling, own, ratio_rows)
    w = (x * 4 + z) * 2 + c
    for step in range(3):
        totals = jnp.sum(to_all(part.reshape(WIDTH)), axis=1)
        total_rows = lax.dynamic_slice_in_dim(totals, w, 1).reshape(WIDTH)
        total_cols = lax.dynamic_slice_in_dim(totals, y * GROUPS, GROUPS)
        if step == 2:
            break
        ratio_rows = visit_rows.reshape(WIDTH) / total_rows
        ratio = ratio_rows[:, None] + (visit_cols / total_cols).reshape(COLS)[None, :]
        part = jnp.sum(sym / ratio, axis=1)
    transition = sym * (STATES / total_rows)[:, None] / ratio
    stationary = STATES * total_rows / jnp.sum(totals)
    return (transition, stationary)


def solution(mesh):
    mesh = Mesh(mesh.devices.reshape(4, 4, 2, 4), ALL)
    return jax.shard_map(
        shards,
        mesh=mesh,
        in_specs=(P("y", WIDE),),
        out_specs=(P(WIDE, "y"), P(WIDE)),
        check_vma=False,
    )
```

```python
import jax
import jax.numpy as jnp
from jax import lax
from jax.experimental import pallas as pl
from jax.experimental.pallas import tpu as pltpu
from jax.sharding import Mesh, PartitionSpec as P


STATES = 8192
TAU = 64
FRAMES = 2048
WIDE = ("x", "z", "c")
ALL = ("x", "z", "c", "y")
BLOCK = 512
WIDTH = 256
COLS = 2048
GROUPS = COLS // WIDTH
FIRST = 256
STACK = 2 * WIDTH + 16
PART = WIDTH + 16
LANES = 128


def place(x, y, z, c):
    return ((x * 4 + z) * 2 + c) * 4 + y


def across():
    return [
        (place(x, y, z, c), place(y, x, z, c))
        for x in range(4) for y in range(4) for z in range(4) for c in range(2)
    ]


def along(k):
    return [(i, (i + k) % 4) for i in range(4)]


def ring(v, axis):
    return [v] + [lax.ppermute(v, axis, along(k)) for k in (1, 2, 3)]


def to_all(sent):
    return lax.all_to_all(sent, ALL, 0, 0).reshape(32, 4, sent.shape[-1])


VMEM = pl.BlockSpec(memory_space=pltpu.VMEM)
SMEM = pl.BlockSpec(memory_space=pltpu.SMEM)


def f32(*shape):
    return jax.ShapeDtypeStruct(shape, jnp.float32)


def row_parts(sym_ref, ratio_rows, ratio_cols):
    parts = []
    for top in range(0, WIDTH, 64):
        acc = jnp.zeros((64, LANES), jnp.float32)
        for k in range(COLS // LANES):
            g, lo = divmod(k * LANES, WIDTH)
            acc += sym_ref[top:top + 64, k * LANES:(k + 1) * LANES] / (
                ratio_rows[top:top + 64] + ratio_cols[g:g + 1, lo:lo + LANES])
        parts.append(acc)
    return jnp.sum(jnp.concatenate(parts, axis=0).T, axis=0, keepdims=True)


def grouped(acc):
    return jnp.concatenate([acc[:WIDTH] + acc[WIDTH:2 * WIDTH], acc[2 * WIDTH:]], axis=0)


def call(kernel, out, *operands):
    return pl.pallas_call(
        kernel,
        in_specs=[SMEM] + [VMEM] * (len(operands) - 1),
        out_specs=[VMEM] * len(out),
        out_shape=out,
        compiler_params=pltpu.CompilerParams(vmem_limit_bytes=16 << 20),
    )(operands[0], *[pltpu.with_memory_space_constraint(v, pltpu.VMEM) for v in operands[1:]])


def left_of(where_ref, left_ref, dx, late):
    lo = lax.rem(where_ref[0] + 4 - dx, 4) * BLOCK + late * FIRST
    return left_ref[:, pl.ds(pl.multiple_of(lo, FIRST), FIRST)]


NEAR = (0, 1, 3)


def near(where, left, by_x, by_z):
    def kernel(where_ref, left_ref, *refs):
        x_refs, z_refs, out_ref = refs[:3], refs[3:6], refs[6]
        for dz in range(4):
            acc = jnp.zeros((STACK, WIDTH), jnp.float32)
            for i, dx in enumerate(NEAR):
                acc += jnp.dot(left_of(where_ref, left_ref, dx, 0), x_refs[i][dz],
                               preferred_element_type=jnp.float32)
            if dz in NEAR:
                for dx in range(4):
                    acc += jnp.dot(left_of(where_ref, left_ref, dx, 1), z_refs[NEAR.index(dz)][dx],
                                   preferred_element_type=jnp.float32)
            out_ref[dz] = grouped(acc)

    return call(kernel, [f32(4, PART, WIDTH)], where, left, *by_x, *by_z)[0]


def far_sums(where_ref, left_ref, x_refs, z_refs, dz):
    acc = jnp.dot(left_of(where_ref, left_ref, 2, 0), x_refs[dz // 2][dz % 2],
                  preferred_element_type=jnp.float32)
    if dz == 2:
        for dx in range(4):
            acc += jnp.dot(left_of(where_ref, left_ref, dx, 1), z_refs[dx // 2][dx % 2],
                           preferred_element_type=jnp.float32)
    return grouped(acc)


def far(where, left, by_x, by_z, so_far):
    def kernel(where_ref, left_ref, xa, xb, za, zb, near_ref, out_ref):
        for dz in range(4):
            out_ref[dz] = near_ref[dz] + far_sums(where_ref, left_ref, (xa, xb), (za, zb), dz)

    return call(kernel, [f32(4, PART, WIDTH)], where, left, *by_x, *by_z, so_far)[0]


def far_and_first(where, left, by_x, by_z, so_far, own, ratio_rows):
    def kernel(where_ref, left_ref, xa, xb, za, zb, near_ref, own_ref, ratio_ref,
               sym_ref, visit_ref, send_ref, total_ref):
        z, c = where_ref[2], where_ref[3]
        for dz in range(4):
            mine = own_ref[dz]
            theirs = near_ref[dz] + far_sums(where_ref, left_ref, (xa, xb), (za, zb), dz)
            for core, part in ((c, mine), (1 - c, theirs)):
                g = lax.rem(z + 4 - dz, 4) * 2 + core
                sym_ref[:, pl.ds(pl.multiple_of(g * WIDTH, WIDTH), WIDTH)] = part[:WIDTH]
                frame = part[WIDTH:]
                visit_ref[pl.ds(g, 1), :] = jnp.sum(frame[:3], axis=0, keepdims=True)
                total_ref[pl.ds(g, 1), :] = jnp.sum(frame[:6], axis=0, keepdims=True)
        sums = row_parts(sym_ref, ratio_ref[...], visit_ref[...] / total_ref[...])
        send_ref[...] = jnp.broadcast_to(sums[None], send_ref.shape)

    out = [f32(WIDTH, COLS), f32(GROUPS, WIDTH), f32(128, 1, WIDTH), f32(GROUPS, WIDTH)]
    return call(kernel, out, where, left, *by_x, *by_z, so_far, own, ratio_rows)[:3]


def three_parts(v):
    hi = v.astype(jnp.bfloat16).astype(jnp.float32)
    mid = (v - hi).astype(jnp.bfloat16).astype(jnp.float32)
    return [hi, mid, v - hi - mid]


def prepare(where, blocks, frames):
    def kernel(where_ref, *refs):
        frame_ref, left_ref, visit_ref, ratio_ref, rows_ref = refs[4:]
        edge = jnp.zeros((TAU, WIDTH), jnp.bfloat16)
        rows_ref[:TAU, :] = edge
        rows_ref[TAU + FRAMES:, :] = edge
        for k in range(4):
            lo = lax.rem(where_ref[1] + k, 4) * BLOCK + TAU
            rows_ref[pl.ds(pl.multiple_of(lo, TAU), BLOCK), :] = refs[k][...]
        for lo in range(0, FRAMES + 2 * TAU, LANES):
            turned = rows_ref[lo:lo + LANES, :].astype(jnp.float32).T.astype(jnp.bfloat16)
            if lo < FRAMES:
                left_ref[:WIDTH, lo:lo + LANES] = turned
            if lo >= 2 * TAU:
                left_ref[WIDTH:2 * WIDTH, lo - 2 * TAU:lo - 2 * TAU + LANES] = turned
        total = jnp.concatenate(
            [jnp.sum(frame_ref[32 * q:32 * q + 32], axis=0) for q in range(4)], axis=1)
        total = jnp.broadcast_to(total, (16, FRAMES))
        at = lax.broadcasted_iota(jnp.int32, (16, FRAMES), 1)
        line = lax.broadcasted_iota(jnp.int32, (16, FRAMES), 0)
        up = jnp.where(at < FRAMES - TAU, pltpu.roll(total, FRAMES - TAU, 1), 0.0)
        down = jnp.where(at >= TAU, pltpu.roll(total, TAU, 1), 0.0)
        weight = jnp.zeros((16, FRAMES), jnp.float32)
        for i, v in enumerate(three_parts(up) + three_parts(down)):
            weight = jnp.where(line == i, v, weight)
        left_ref[2 * WIDTH:, :] = weight.astype(jnp.bfloat16)
        weight = jnp.zeros((16, FRAMES), jnp.float32)
        for i, v in enumerate(three_parts(total)):
            weight = jnp.where(line == i, v, weight)
        weight = weight.astype(jnp.bfloat16)
        visit = jnp.sum(jnp.dot(weight, rows_ref[:FRAMES, :], preferred_element_type=jnp.float32),
                        axis=0, keepdims=True)
        back = jnp.sum(jnp.dot(weight, rows_ref[2 * TAU:, :], preferred_element_type=jnp.float32),
                       axis=0, keepdims=True)
        visit_ref[...] = visit
        ratio_ref[...] = jnp.broadcast_to(visit / (visit + back), (LANES, WIDTH)).T

    return pl.pallas_call(
        kernel,
        in_specs=[SMEM] + [VMEM] * 5,
        out_specs=[VMEM] * 3,
        out_shape=[jax.ShapeDtypeStruct((STACK, FRAMES), jnp.bfloat16), f32(1, WIDTH), f32(WIDTH, LANES)],
        scratch_shapes=[pltpu.VMEM((FRAMES + 2 * TAU, WIDTH), jnp.bfloat16)],
        compiler_params=pltpu.CompilerParams(vmem_limit_bytes=16 << 20),
    )(where, *[pltpu.with_memory_space_constraint(v, pltpu.VMEM) for v in blocks + [frames]])


def from_sides(v, axis):
    return [lax.ppermute(v, axis, along(k)) for k in (1, 3)]


def from_afar(where, sides, axis):
    def cut(_, back_ref, on_ref, first_ref, second_ref):
        first_ref[...] = back_ref[:2]
        second_ref[...] = on_ref[2:]

    half = jax.ShapeDtypeStruct((2,) + sides[0].shape[1:], sides[0].dtype)
    halves = call(cut, [half, half], where, *sides)
    return [lax.ppermute(halves[0], axis, along(1)), lax.ppermute(halves[1], axis, along(3))]


def swapped(vs):
    return [lax.ppermute(v, "c", [(0, 1), (1, 0)]) for v in vs]


def shards(member):
    where = jnp.stack([lax.axis_index(a) for a in ("x", "y", "z", "c")])
    x, y, z, c = (where[i] for i in range(4))
    moved = lax.ppermute(member, ALL, across())
    part = jnp.sum(member, axis=1, dtype=jnp.float32)
    part, where = lax.optimization_barrier((part, where))
    frames = lax.all_to_all(jnp.broadcast_to(part, (128, 1, BLOCK)), ("y",) + WIDE, 0, 0)
    once_x = jnp.stack(ring(moved[:FIRST], "z"))
    once_z = jnp.stack(ring(moved[FIRST:], "x"))
    near_x = from_sides(once_x, "x")
    near_z = from_sides(once_z, "z")
    far_x = from_afar(where, near_x, "x")
    far_z = from_afar(where, near_z, "z")
    kept, frames = lax.optimization_barrier((member, frames))
    blocks = [member] + [lax.ppermute(kept, "y", along(-k)) for k in (1, 2, 3)]
    left, visit_rows, ratio_rows = prepare(where, blocks, frames)
    own = near(where, left, [once_x] + near_x, [once_z] + near_z)
    once_x, once_z = swapped([once_x, once_z])
    near_x, near_z = swapped(near_x), swapped(near_z)
    sibling = near(where, left, [once_x] + near_x, [once_z] + near_z)
    own = far(where, left, far_x, far_z, own)
    far_x, far_z = swapped(far_x), swapped(far_z)
    sym, visit_cols, send = far_and_first(where, left, far_x, far_z, sibling, own, ratio_rows)
    w = (x * 4 + z) * 2 + c
    for step in range(3):
        totals = jnp.sum(to_all(send), axis=1)
        total_rows = lax.dynamic_slice_in_dim(totals, w, 1).reshape(WIDTH)
        total_cols = lax.dynamic_slice_in_dim(totals, y * GROUPS, GROUPS)
        if step == 2:
            break
        ratio_rows = visit_rows.reshape(WIDTH) / total_rows
        ratio = ratio_rows[:, None] + (visit_cols / total_cols).reshape(COLS)[None, :]
        send = jnp.broadcast_to(jnp.sum(sym / ratio, axis=1), (128, 1, WIDTH))
    transition = sym * (STATES / total_rows)[:, None] / ratio
    stationary = STATES * total_rows / jnp.sum(totals)
    return (transition, stationary)


def solution(mesh):
    mesh = Mesh(mesh.devices.reshape(4, 4, 2, 4), ALL)
    return jax.shard_map(
        shards,
        mesh=mesh,
        in_specs=(P("y", WIDE),),
        out_specs=(P(WIDE, "y"), P(WIDE)),
        check_vma=False,
    )
```

```python
import jax
import jax.numpy as jnp
from jax import lax
from jax.experimental import pallas as pl
from jax.experimental.pallas import tpu as pltpu
from jax.sharding import Mesh, PartitionSpec as P


STATES = 8192
TAU = 64
FRAMES = 2048
WIDE = ("x", "z", "c")
ALL = ("x", "z", "c", "y")
BLOCK = 512
WIDTH = 256
COLS = 2048
GROUPS = COLS // WIDTH
FIRST = 256
STACK = 2 * WIDTH + 16
PART = WIDTH + 16
LANES = 128


def place(x, y, z, c):
    return ((x * 4 + z) * 2 + c) * 4 + y


def across():
    return [
        (place(x, y, z, c), place(y, x, z, c))
        for x in range(4) for y in range(4) for z in range(4) for c in range(2)
    ]


def along(k):
    return [(i, (i + k) % 4) for i in range(4)]


def ring(v, axis):
    return [v] + [lax.ppermute(v, axis, along(k)) for k in (1, 2, 3)]


def to_all(sent):
    return lax.all_to_all(sent, ("y",) + WIDE, 0, 0)


VMEM = pl.BlockSpec(memory_space=pltpu.VMEM)
SMEM = pl.BlockSpec(memory_space=pltpu.SMEM)


def f32(*shape):
    return jax.ShapeDtypeStruct(shape, jnp.float32)


def row_parts(sym_ref, ratio_rows, ratio_cols):
    parts = []
    for top in range(0, WIDTH, 64):
        acc = jnp.zeros((64, LANES), jnp.float32)
        for k in range(COLS // LANES):
            g, lo = divmod(k * LANES, WIDTH)
            acc += sym_ref[top:top + 64, k * LANES:(k + 1) * LANES] / (
                ratio_rows[top:top + 64] + ratio_cols[g:g + 1, lo:lo + LANES])
        parts.append(acc)
    return jnp.sum(jnp.concatenate(parts, axis=0).T, axis=0, keepdims=True)


def grouped(acc):
    return jnp.concatenate([acc[:WIDTH] + acc[WIDTH:2 * WIDTH], acc[2 * WIDTH:]], axis=0)


def call(kernel, out, *operands):
    return pl.pallas_call(
        kernel,
        in_specs=[SMEM] + [VMEM] * (len(operands) - 1),
        out_specs=[VMEM] * len(out),
        out_shape=out,
        compiler_params=pltpu.CompilerParams(vmem_limit_bytes=16 << 20),
    )(operands[0], *[pltpu.with_memory_space_constraint(v, pltpu.VMEM) for v in operands[1:]])


def left_of(where_ref, left_ref, dx, late):
    lo = lax.rem(where_ref[0] + 4 - dx, 4) * BLOCK + late * FIRST
    return left_ref[:, pl.ds(pl.multiple_of(lo, FIRST), FIRST)]


NEAR = (0, 1, 3)


def near(where, left, by_x, by_z):
    def kernel(where_ref, left_ref, *refs):
        x_refs, z_refs, out_ref = refs[:3], refs[3:6], refs[6]
        for dz in range(4):
            acc = jnp.zeros((STACK, WIDTH), jnp.float32)
            for i, dx in enumerate(NEAR):
                acc += jnp.dot(left_of(where_ref, left_ref, dx, 0), x_refs[i][dz],
                               preferred_element_type=jnp.float32)
            if dz in NEAR:
                for dx in range(4):
                    acc += jnp.dot(left_of(where_ref, left_ref, dx, 1), z_refs[NEAR.index(dz)][dx],
                                   preferred_element_type=jnp.float32)
            out_ref[dz] = grouped(acc)

    return call(kernel, [f32(4, PART, WIDTH)], where, left, *by_x, *by_z)[0]


def far_sums(where_ref, left_ref, x_refs, z_refs, dz):
    acc = jnp.dot(left_of(where_ref, left_ref, 2, 0), x_refs[dz // 2][dz % 2],
                  preferred_element_type=jnp.float32)
    if dz == 2:
        for dx in range(4):
            acc += jnp.dot(left_of(where_ref, left_ref, dx, 1), z_refs[dx // 2][dx % 2],
                           preferred_element_type=jnp.float32)
    return grouped(acc)


def far(where, left, by_x, by_z, so_far):
    def kernel(where_ref, left_ref, xa, xb, za, zb, near_ref, out_ref):
        for dz in range(4):
            out_ref[dz] = near_ref[dz] + far_sums(where_ref, left_ref, (xa, xb), (za, zb), dz)

    return call(kernel, [f32(4, PART, WIDTH)], where, left, *by_x, *by_z, so_far)[0]


def far_and_first(where, left, by_x, by_z, so_far, own, ratio_rows):
    def kernel(where_ref, left_ref, xa, xb, za, zb, near_ref, own_ref, ratio_ref,
               sym_ref, visit_ref, send_ref, total_ref):
        z, c = where_ref[2], where_ref[3]
        for dz in range(4):
            mine = own_ref[dz]
            theirs = near_ref[dz] + far_sums(where_ref, left_ref, (xa, xb), (za, zb), dz)
            for core, part in ((c, mine), (1 - c, theirs)):
                g = lax.rem(z + 4 - dz, 4) * 2 + core
                sym_ref[:, pl.ds(pl.multiple_of(g * WIDTH, WIDTH), WIDTH)] = part[:WIDTH]
                frame = part[WIDTH:]
                visit_ref[pl.ds(g, 1), :] = jnp.sum(frame[:3], axis=0, keepdims=True)
                total_ref[pl.ds(g, 1), :] = jnp.sum(frame[:6], axis=0, keepdims=True)
        sums = row_parts(sym_ref, ratio_ref[...], visit_ref[...] / total_ref[...])
        send_ref[...] = jnp.broadcast_to(sums[None], send_ref.shape)

    out = [f32(WIDTH, COLS), f32(GROUPS, WIDTH), f32(128, 1, WIDTH), f32(GROUPS, WIDTH)]
    return call(kernel, out, where, left, *by_x, *by_z, so_far, own, ratio_rows)[:3]


def three_parts(v):
    hi = v.astype(jnp.bfloat16).astype(jnp.float32)
    mid = (v - hi).astype(jnp.bfloat16).astype(jnp.float32)
    return [hi, mid, v - hi - mid]


def prepare(where, blocks, frames):
    def kernel(where_ref, *refs):
        frame_ref, left_ref, visit_ref, ratio_ref, rows_ref = refs[4:]
        edge = jnp.zeros((TAU, WIDTH), jnp.bfloat16)
        rows_ref[:TAU, :] = edge
        rows_ref[TAU + FRAMES:, :] = edge
        for k in range(4):
            lo = lax.rem(where_ref[1] + k, 4) * BLOCK + TAU
            rows_ref[pl.ds(pl.multiple_of(lo, TAU), BLOCK), :] = refs[k][...]
        for lo in range(0, FRAMES + 2 * TAU, LANES):
            turned = rows_ref[lo:lo + LANES, :].astype(jnp.float32).T.astype(jnp.bfloat16)
            if lo < FRAMES:
                left_ref[:WIDTH, lo:lo + LANES] = turned
            if lo >= 2 * TAU:
                left_ref[WIDTH:2 * WIDTH, lo - 2 * TAU:lo - 2 * TAU + LANES] = turned
        total = jnp.concatenate(
            [jnp.sum(frame_ref[32 * q:32 * q + 32], axis=0) for q in range(4)], axis=1)
        total = jnp.broadcast_to(total, (16, FRAMES))
        at = lax.broadcasted_iota(jnp.int32, (16, FRAMES), 1)
        line = lax.broadcasted_iota(jnp.int32, (16, FRAMES), 0)
        up = jnp.where(at < FRAMES - TAU, pltpu.roll(total, FRAMES - TAU, 1), 0.0)
        down = jnp.where(at >= TAU, pltpu.roll(total, TAU, 1), 0.0)
        weight = jnp.zeros((16, FRAMES), jnp.float32)
        for i, v in enumerate(three_parts(up) + three_parts(down)):
            weight = jnp.where(line == i, v, weight)
        left_ref[2 * WIDTH:, :] = weight.astype(jnp.bfloat16)
        weight = jnp.zeros((16, FRAMES), jnp.float32)
        for i, v in enumerate(three_parts(total)):
            weight = jnp.where(line == i, v, weight)
        weight = weight.astype(jnp.bfloat16)
        visit = jnp.sum(jnp.dot(weight, rows_ref[:FRAMES, :], preferred_element_type=jnp.float32),
                        axis=0, keepdims=True)
        back = jnp.sum(jnp.dot(weight, rows_ref[2 * TAU:, :], preferred_element_type=jnp.float32),
                       axis=0, keepdims=True)
        visit_ref[...] = visit
        ratio_ref[...] = jnp.broadcast_to(visit / (visit + back), (LANES, WIDTH)).T

    return pl.pallas_call(
        kernel,
        in_specs=[SMEM] + [VMEM] * 5,
        out_specs=[VMEM] * 3,
        out_shape=[jax.ShapeDtypeStruct((STACK, FRAMES), jnp.bfloat16), f32(1, WIDTH), f32(WIDTH, LANES)],
        scratch_shapes=[pltpu.VMEM((FRAMES + 2 * TAU, WIDTH), jnp.bfloat16)],
        compiler_params=pltpu.CompilerParams(vmem_limit_bytes=16 << 20),
    )(where, *[pltpu.with_memory_space_constraint(v, pltpu.VMEM) for v in blocks + [frames]])


def from_sides(v, axis):
    return [lax.ppermute(v, axis, along(k)) for k in (1, 3)]


def from_afar(where, sides, axis):
    def cut(_, back_ref, on_ref, first_ref, second_ref):
        first_ref[...] = back_ref[:2]
        second_ref[...] = on_ref[2:]

    half = jax.ShapeDtypeStruct((2,) + sides[0].shape[1:], sides[0].dtype)
    halves = call(cut, [half, half], where, *sides)
    return [lax.ppermute(halves[0], axis, along(1)), lax.ppermute(halves[1], axis, along(3))]


def swapped(vs):
    return [lax.ppermute(v, "c", [(0, 1), (1, 0)]) for v in vs]


def finish(where, got, last, sym, visit_cols, visit_rows):
    def kernel(where_ref, got_ref, last_ref, sym_ref, visit_col_ref, visit_row_ref,
               out_ref, share_ref, total_ref, row_ref, scale_ref):
        g = pl.program_id(0)
        x, y, z, c = (where_ref[i] for i in range(4))

        @pl.when(g == 0)
        def _():
            w = (x * 4 + z) * 2 + c
            total_ref[...] = sum(last_ref[32 * k:32 * k + 32] for k in range(4))
            own = total_ref[w]
            scale_ref[...] = jnp.broadcast_to(STATES / own, (LANES, WIDTH)).T
            grand = jnp.sum(jnp.sum(total_ref[...], axis=0), axis=1, keepdims=True)
            share_ref[...] = STATES * own / grand
            total_ref[...] = sum(got_ref[32 * k:32 * k + 32] for k in range(4))
            row_ref[...] = jnp.broadcast_to(visit_row_ref[...] / total_ref[w], (LANES, WIDTH)).T

        col = visit_col_ref[pl.ds(g, 1), :] / total_ref[y * GROUPS + g]
        for lo in range(0, WIDTH, LANES):
            out_ref[:, lo:lo + LANES] = scale_ref[...] * sym_ref[:, lo:lo + LANES] / (
                row_ref[...] + col[:, lo:lo + LANES])

    return pl.pallas_call(
        kernel,
        grid=(GROUPS,),
        in_specs=[SMEM, VMEM, VMEM, pl.BlockSpec((WIDTH, WIDTH), lambda g: (0, g)), VMEM, VMEM],
        out_specs=[pl.BlockSpec((WIDTH, WIDTH), lambda g: (0, g)),
                   pl.BlockSpec((1, WIDTH), lambda g: (0, 0))],
        out_shape=[f32(WIDTH, COLS), f32(1, WIDTH)],
        scratch_shapes=[pltpu.VMEM((32, 1, WIDTH), jnp.float32)] + [pltpu.VMEM((WIDTH, LANES), jnp.float32)] * 2,
        compiler_params=pltpu.CompilerParams(vmem_limit_bytes=16 << 20),
    )(where, got, last, sym, visit_cols, visit_rows)


def shards(member):
    where = jnp.stack([lax.axis_index(a) for a in ("x", "y", "z", "c")])
    x, y, z, c = (where[i] for i in range(4))
    moved = lax.ppermute(member, ALL, across())
    part = jnp.sum(member, axis=1, dtype=jnp.float32)
    part, where = lax.optimization_barrier((part, where))
    frames = to_all(jnp.broadcast_to(part, (128, 1, BLOCK)))
    once_x = jnp.stack(ring(moved[:FIRST], "z"))
    once_z = jnp.stack(ring(moved[FIRST:], "x"))
    near_x = from_sides(once_x, "x")
    near_z = from_sides(once_z, "z")
    far_x = from_afar(where, near_x, "x")
    far_z = from_afar(where, near_z, "z")
    kept, frames = lax.optimization_barrier((member, frames))
    blocks = [member] + [lax.ppermute(kept, "y", along(-k)) for k in (1, 2, 3)]
    left, visit_rows, ratio_rows = prepare(where, blocks, frames)
    own = near(where, left, [once_x] + near_x, [once_z] + near_z)
    once_x, once_z = swapped([once_x, once_z])
    near_x, near_z = swapped(near_x), swapped(near_z)
    sibling = near(where, left, [once_x] + near_x, [once_z] + near_z)
    own = far(where, left, far_x, far_z, own)
    far_x, far_z = swapped(far_x), swapped(far_z)
    sym, visit_cols, send = far_and_first(where, left, far_x, far_z, sibling, own, ratio_rows)
    w, first = (x * 4 + z) * 2 + c, y * GROUPS
    for _ in range(2):
        got = to_all(send)
        totals = jnp.sum(got.reshape(4, 32, WIDTH), axis=0)
        total_rows = lax.dynamic_slice_in_dim(totals, w, 1).reshape(WIDTH)
        total_cols = lax.dynamic_slice_in_dim(totals, first, GROUPS)
        ratio_rows = visit_rows.reshape(WIDTH) / total_rows
        ratio = ratio_rows[:, None] + (visit_cols / total_cols).reshape(COLS)[None, :]
        send = jnp.broadcast_to(jnp.sum(sym / ratio, axis=1), (128, 1, WIDTH))
    transition, stationary = finish(where, got, to_all(send), sym, visit_cols, visit_rows)
    return (transition, stationary.reshape(WIDTH))


def solution(mesh):
    mesh = Mesh(mesh.devices.reshape(4, 4, 2, 4), ALL)
    return jax.shard_map(
        shards,
        mesh=mesh,
        in_specs=(P("y", WIDE),),
        out_specs=(P(WIDE, "y"), P(WIDE)),
        check_vma=False,
    )
```

```python
import jax
import jax.numpy as jnp
from jax import lax
from jax.experimental import pallas as pl
from jax.experimental.pallas import tpu as pltpu
from jax.sharding import Mesh, PartitionSpec as P


STATES = 8192
TAU = 64
FRAMES = 2048
WIDE = ("x", "z", "c")
ALL = ("x", "z", "c", "y")
BLOCK = 512
WIDTH = 256
COLS = 2048
GROUPS = COLS // WIDTH
FIRST = 256
STACK = 2 * WIDTH + 16
PART = WIDTH + 16
LANES = 128
ROWS = 64


def place(x, y, z, c):
    return ((x * 4 + z) * 2 + c) * 4 + y


def across():
    return [
        (place(x, y, z, c), place(y, x, z, c))
        for x in range(4) for y in range(4) for z in range(4) for c in range(2)
    ]


def along(k):
    return [(i, (i + k) % 4) for i in range(4)]


def ring(v, axis):
    return [v] + [lax.ppermute(v, axis, along(k)) for k in (1, 2, 3)]


def to_all(sent):
    return lax.all_to_all(sent, ("y",) + WIDE, 0, 0)


VMEM = pl.BlockSpec(memory_space=pltpu.VMEM)
SMEM = pl.BlockSpec(memory_space=pltpu.SMEM)


def f32(*shape):
    return jax.ShapeDtypeStruct(shape, jnp.float32)


def row_parts(sym_ref, ratio_rows, ratio_cols):
    parts = []
    for top in range(0, WIDTH, 64):
        acc = jnp.zeros((64, LANES), jnp.float32)
        for k in range(COLS // LANES):
            g, lo = divmod(k * LANES, WIDTH)
            acc += sym_ref[top:top + 64, k * LANES:(k + 1) * LANES] / (
                ratio_rows[top:top + 64] + ratio_cols[g:g + 1, lo:lo + LANES])
        parts.append(acc)
    return jnp.sum(jnp.concatenate(parts, axis=0).T, axis=0, keepdims=True)


def grouped(acc):
    return jnp.concatenate([acc[:WIDTH] + acc[WIDTH:2 * WIDTH], acc[2 * WIDTH:]], axis=0)


def call(kernel, out, *operands):
    return pl.pallas_call(
        kernel,
        in_specs=[SMEM] + [VMEM] * (len(operands) - 1),
        out_specs=[VMEM] * len(out),
        out_shape=out,
        compiler_params=pltpu.CompilerParams(vmem_limit_bytes=16 << 20),
    )(operands[0], *[pltpu.with_memory_space_constraint(v, pltpu.VMEM) for v in operands[1:]])


def left_of(where_ref, left_ref, dx, late):
    lo = lax.rem(where_ref[0] + 4 - dx, 4) * BLOCK + late * FIRST
    return left_ref[:, pl.ds(pl.multiple_of(lo, FIRST), FIRST)]


NEAR = (0, 1, 3)


def near(where, left, by_x, by_z):
    def kernel(where_ref, left_ref, *refs):
        x_refs, z_refs, out_ref = refs[:3], refs[3:6], refs[6]
        for dz in range(4):
            acc = jnp.zeros((STACK, WIDTH), jnp.float32)
            for i, dx in enumerate(NEAR):
                acc += jnp.dot(left_of(where_ref, left_ref, dx, 0), x_refs[i][dz],
                               preferred_element_type=jnp.float32)
            if dz in NEAR:
                for dx in range(4):
                    acc += jnp.dot(left_of(where_ref, left_ref, dx, 1), z_refs[NEAR.index(dz)][dx],
                                   preferred_element_type=jnp.float32)
            out_ref[dz] = grouped(acc)

    return call(kernel, [f32(4, PART, WIDTH)], where, left, *by_x, *by_z)[0]


def far_sums(where_ref, left_ref, x_refs, z_refs, dz):
    acc = jnp.dot(left_of(where_ref, left_ref, 2, 0), x_refs[dz // 2][dz % 2],
                  preferred_element_type=jnp.float32)
    if dz == 2:
        for dx in range(4):
            acc += jnp.dot(left_of(where_ref, left_ref, dx, 1), z_refs[dx // 2][dx % 2],
                           preferred_element_type=jnp.float32)
    return grouped(acc)


def far(where, left, by_x, by_z, so_far):
    def kernel(where_ref, left_ref, xa, xb, za, zb, near_ref, out_ref):
        for dz in range(4):
            out_ref[dz] = near_ref[dz] + far_sums(where_ref, left_ref, (xa, xb), (za, zb), dz)

    return call(kernel, [f32(4, PART, WIDTH)], where, left, *by_x, *by_z, so_far)[0]


def far_and_first(where, left, by_x, by_z, so_far, own, ratio_rows):
    def kernel(where_ref, left_ref, xa, xb, za, zb, near_ref, own_ref, ratio_ref,
               sym_ref, visit_ref, send_ref, total_ref):
        z, c = where_ref[2], where_ref[3]
        for dz in range(4):
            mine = own_ref[dz]
            theirs = near_ref[dz] + far_sums(where_ref, left_ref, (xa, xb), (za, zb), dz)
            for core, part in ((c, mine), (1 - c, theirs)):
                g = lax.rem(z + 4 - dz, 4) * 2 + core
                sym_ref[:, pl.ds(pl.multiple_of(g * WIDTH, WIDTH), WIDTH)] = part[:WIDTH]
                frame = part[WIDTH:]
                visit_ref[pl.ds(g, 1), :] = jnp.sum(frame[:3], axis=0, keepdims=True)
                total_ref[pl.ds(g, 1), :] = jnp.sum(frame[:6], axis=0, keepdims=True)
        sums = row_parts(sym_ref, ratio_ref[...], visit_ref[...] / total_ref[...])
        send_ref[...] = jnp.broadcast_to(sums[None], send_ref.shape)

    out = [f32(WIDTH, COLS), f32(GROUPS, WIDTH), f32(128, 1, WIDTH), f32(GROUPS, WIDTH)]
    return call(kernel, out, where, left, *by_x, *by_z, so_far, own, ratio_rows)[:3]


def three_parts(v):
    hi = v.astype(jnp.bfloat16).astype(jnp.float32)
    mid = (v - hi).astype(jnp.bfloat16).astype(jnp.float32)
    return [hi, mid, v - hi - mid]


def prepare(where, blocks, frames):
    def kernel(where_ref, *refs):
        frame_ref, left_ref, visit_ref, ratio_ref, rows_ref = refs[4:]
        edge = jnp.zeros((TAU, WIDTH), jnp.bfloat16)
        rows_ref[:TAU, :] = edge
        rows_ref[TAU + FRAMES:, :] = edge
        for k in range(4):
            lo = lax.rem(where_ref[1] + k, 4) * BLOCK + TAU
            rows_ref[pl.ds(pl.multiple_of(lo, TAU), BLOCK), :] = refs[k][...]
        for lo in range(0, FRAMES + 2 * TAU, LANES):
            turned = rows_ref[lo:lo + LANES, :].astype(jnp.float32).T.astype(jnp.bfloat16)
            if lo < FRAMES:
                left_ref[:WIDTH, lo:lo + LANES] = turned
            if lo >= 2 * TAU:
                left_ref[WIDTH:2 * WIDTH, lo - 2 * TAU:lo - 2 * TAU + LANES] = turned
        total = jnp.concatenate(
            [jnp.sum(frame_ref[32 * q:32 * q + 32], axis=0) for q in range(4)], axis=1)
        total = jnp.broadcast_to(total, (16, FRAMES))
        at = lax.broadcasted_iota(jnp.int32, (16, FRAMES), 1)
        line = lax.broadcasted_iota(jnp.int32, (16, FRAMES), 0)
        up = jnp.where(at < FRAMES - TAU, pltpu.roll(total, FRAMES - TAU, 1), 0.0)
        down = jnp.where(at >= TAU, pltpu.roll(total, TAU, 1), 0.0)
        weight = jnp.zeros((16, FRAMES), jnp.float32)
        for i, v in enumerate(three_parts(up) + three_parts(down)):
            weight = jnp.where(line == i, v, weight)
        left_ref[2 * WIDTH:, :] = weight.astype(jnp.bfloat16)
        weight = jnp.zeros((16, FRAMES), jnp.float32)
        for i, v in enumerate(three_parts(total)):
            weight = jnp.where(line == i, v, weight)
        weight = weight.astype(jnp.bfloat16)
        visit = jnp.sum(jnp.dot(weight, rows_ref[:FRAMES, :], preferred_element_type=jnp.float32),
                        axis=0, keepdims=True)
        back = jnp.sum(jnp.dot(weight, rows_ref[2 * TAU:, :], preferred_element_type=jnp.float32),
                       axis=0, keepdims=True)
        visit_ref[...] = visit
        ratio_ref[...] = jnp.broadcast_to(visit / (visit + back), (LANES, WIDTH)).T

    return pl.pallas_call(
        kernel,
        in_specs=[SMEM] + [VMEM] * 5,
        out_specs=[VMEM] * 3,
        out_shape=[jax.ShapeDtypeStruct((STACK, FRAMES), jnp.bfloat16), f32(1, WIDTH), f32(WIDTH, LANES)],
        scratch_shapes=[pltpu.VMEM((FRAMES + 2 * TAU, WIDTH), jnp.bfloat16)],
        compiler_params=pltpu.CompilerParams(vmem_limit_bytes=16 << 20),
    )(where, *[pltpu.with_memory_space_constraint(v, pltpu.VMEM) for v in blocks + [frames]])


def from_sides(v, axis):
    return [lax.ppermute(v, axis, along(k)) for k in (1, 3)]


def from_afar(where, sides, axis):
    def cut(_, back_ref, on_ref, first_ref, second_ref):
        first_ref[...] = back_ref[:2]
        second_ref[...] = on_ref[2:]

    half = jax.ShapeDtypeStruct((2,) + sides[0].shape[1:], sides[0].dtype)
    halves = call(cut, [half, half], where, *sides)
    return [lax.ppermute(halves[0], axis, along(1)), lax.ppermute(halves[1], axis, along(3))]


def swapped(vs):
    return [lax.ppermute(v, "c", [(0, 1), (1, 0)]) for v in vs]


def finish(where, got, last, sym, visit_cols, visit_rows):
    def kernel(where_ref, got_ref, last_ref, sym_ref, visit_col_ref, visit_row_ref,
               out_ref, share_ref, total_ref, row_ref, scale_ref, col_ref):
        step = pl.program_id(0)
        x, y, z, c = (where_ref[i] for i in range(4))

        @pl.when(step == 0)
        def _():
            w = (x * 4 + z) * 2 + c
            total_ref[...] = sum(last_ref[32 * k:32 * k + 32] for k in range(4))
            own = total_ref[w]
            scale_ref[...] = jnp.broadcast_to(STATES / own, (LANES, WIDTH)).T
            grand = jnp.sum(jnp.sum(total_ref[...], axis=0), axis=1, keepdims=True)
            share_ref[...] = STATES * own / grand
            total_ref[...] = sum(got_ref[32 * k:32 * k + 32] for k in range(4))
            row_ref[...] = jnp.broadcast_to(visit_row_ref[...] / total_ref[w], (LANES, WIDTH)).T
            for g in range(GROUPS):
                col_ref[g:g + 1, :] = visit_col_ref[g:g + 1, :] / total_ref[y * GROUPS + g]

        rows = pl.ds(pl.multiple_of(step * ROWS, ROWS), ROWS)
        for k in range(COLS // LANES):
            lo = k * LANES
            g, at = divmod(lo, WIDTH)
            out_ref[:, lo:lo + LANES] = scale_ref[rows, :] * sym_ref[:, lo:lo + LANES] / (
                row_ref[rows, :] + col_ref[g:g + 1, at:at + LANES])

    block = pl.BlockSpec((ROWS, COLS), lambda i: (i, 0))
    return pl.pallas_call(
        kernel,
        grid=(WIDTH // ROWS,),
        in_specs=[SMEM, VMEM, VMEM, block, VMEM, VMEM],
        out_specs=[block, pl.BlockSpec((1, WIDTH), lambda i: (0, 0))],
        out_shape=[f32(WIDTH, COLS), f32(1, WIDTH)],
        scratch_shapes=[pltpu.VMEM((32, 1, WIDTH), jnp.float32)]
        + [pltpu.VMEM((WIDTH, LANES), jnp.float32)] * 2 + [pltpu.VMEM((GROUPS, WIDTH), jnp.float32)],
        compiler_params=pltpu.CompilerParams(vmem_limit_bytes=16 << 20),
    )(where, got, last, sym, visit_cols, visit_rows)


def shards(member):
    x, y, z, c = (lax.axis_index(a) for a in ("x", "y", "z", "c"))
    where = jnp.stack([x, y, z, c])
    moved = lax.ppermute(member, ALL, across())
    part = jnp.sum(member, axis=1, dtype=jnp.float32)
    w, first = (v.astype(jnp.uint32) for v in ((x * 4 + z) * 2 + c, y * GROUPS))
    part, where, w, first = lax.optimization_barrier((part, where, w, first))
    frames = to_all(jnp.broadcast_to(part, (128, 1, BLOCK)))
    once_x = jnp.stack(ring(moved[:FIRST], "z"))
    once_z = jnp.stack(ring(moved[FIRST:], "x"))
    near_x = from_sides(once_x, "x")
    near_z = from_sides(once_z, "z")
    far_x = from_afar(where, near_x, "x")
    far_z = from_afar(where, near_z, "z")
    kept, frames = lax.optimization_barrier((member, frames))
    blocks = [member] + [lax.ppermute(kept, "y", along(-k)) for k in (1, 2, 3)]
    left, visit_rows, ratio_rows = prepare(where, blocks, frames)
    own = near(where, left, [once_x] + near_x, [once_z] + near_z)
    once_x, once_z = swapped([once_x, once_z])
    near_x, near_z = swapped(near_x), swapped(near_z)
    sibling = near(where, left, [once_x] + near_x, [once_z] + near_z)
    own = far(where, left, far_x, far_z, own)
    far_x, far_z = swapped(far_x), swapped(far_z)
    sym, visit_cols, send = far_and_first(where, left, far_x, far_z, sibling, own, ratio_rows)
    for _ in range(2):
        got = to_all(send)
        totals = jnp.sum(got.reshape(4, 32, WIDTH), axis=0)
        total_rows = lax.dynamic_slice(totals, (w, jnp.uint32(0)), (1, WIDTH)).reshape(WIDTH)
        total_cols = lax.dynamic_slice(totals, (first, jnp.uint32(0)), (GROUPS, WIDTH))
        ratio_rows = visit_rows.reshape(WIDTH) / total_rows
        ratio = ratio_rows[:, None] + (visit_cols / total_cols).reshape(COLS)[None, :]
        send = jnp.broadcast_to(jnp.sum(sym / ratio, axis=1), (128, 1, WIDTH))
    transition, stationary = finish(where, got, to_all(send), sym, visit_cols, visit_rows)
    return (transition, stationary.reshape(WIDTH))


def solution(mesh):
    mesh = Mesh(mesh.devices.reshape(4, 4, 2, 4), ALL)
    return jax.shard_map(
        shards,
        mesh=mesh,
        in_specs=(P("y", WIDE),),
        out_specs=(P(WIDE, "y"), P(WIDE)),
        check_vma=False,
    )
```

```python
import jax
import jax.numpy as jnp
from jax import lax
from jax.experimental import pallas as pl
from jax.experimental.pallas import tpu as pltpu
from jax.sharding import Mesh, PartitionSpec as P


STATES = 8192
TAU = 64
FRAMES = 2048
WIDE = ("x", "z", "c")
ALL = ("x", "z", "c", "y")
BLOCK = 512
WIDTH = 256
COLS = 2048
GROUPS = COLS // WIDTH
FIRST = 256
STACK = 2 * WIDTH + 16
PART = WIDTH + 16
LANES = 128
ROWS = 64


def place(x, y, z, c):
    return ((x * 4 + z) * 2 + c) * 4 + y


def across():
    return [
        (place(x, y, z, c), place(y, x, z, c))
        for x in range(4) for y in range(4) for z in range(4) for c in range(2)
    ]


def along(k):
    return [(i, (i + k) % 4) for i in range(4)]


def ring(v, axis):
    return [v] + [lax.ppermute(v, axis, along(k)) for k in (1, 2, 3)]


def to_all(sent):
    return lax.all_to_all(sent, ("y",) + WIDE, 0, 0)


VMEM = pl.BlockSpec(memory_space=pltpu.VMEM)
SMEM = pl.BlockSpec(memory_space=pltpu.SMEM)


def f32(*shape):
    return jax.ShapeDtypeStruct(shape, jnp.float32)


def row_parts(sym_ref, ratio_rows, ratio_cols):
    parts = []
    for top in range(0, WIDTH, 64):
        acc = jnp.zeros((64, LANES), jnp.float32)
        for k in range(COLS // LANES):
            g, lo = divmod(k * LANES, WIDTH)
            acc += sym_ref[top:top + 64, k * LANES:(k + 1) * LANES] / (
                ratio_rows[top:top + 64] + ratio_cols[g:g + 1, lo:lo + LANES])
        parts.append(acc)
    return jnp.sum(jnp.concatenate(parts, axis=0).T, axis=0, keepdims=True)


def grouped(acc):
    return jnp.concatenate([acc[:WIDTH] + acc[WIDTH:2 * WIDTH], acc[2 * WIDTH:]], axis=0)


def call(kernel, out, *operands):
    return pl.pallas_call(
        kernel,
        in_specs=[SMEM] + [VMEM] * (len(operands) - 1),
        out_specs=[VMEM] * len(out),
        out_shape=out,
        compiler_params=pltpu.CompilerParams(vmem_limit_bytes=16 << 20),
    )(operands[0], *[pltpu.with_memory_space_constraint(v, pltpu.VMEM) for v in operands[1:]])


def left_of(where_ref, left_ref, dx, late):
    lo = lax.rem(where_ref[0] + 4 - dx, 4) * BLOCK + late * FIRST
    return left_ref[:, pl.ds(pl.multiple_of(lo, FIRST), FIRST)]


NEAR = (0, 1, 3)


def near(where, left, by_x, by_z):
    def kernel(where_ref, left_ref, *refs):
        x_refs, z_refs, out_ref = refs[:3], refs[3:6], refs[6]
        for dz in range(4):
            acc = jnp.zeros((STACK, WIDTH), jnp.float32)
            for i, dx in enumerate(NEAR):
                acc += jnp.dot(left_of(where_ref, left_ref, dx, 0), x_refs[i][dz],
                               preferred_element_type=jnp.float32)
            if dz in NEAR:
                for dx in range(4):
                    acc += jnp.dot(left_of(where_ref, left_ref, dx, 1), z_refs[NEAR.index(dz)][dx],
                                   preferred_element_type=jnp.float32)
            out_ref[dz] = grouped(acc)

    return call(kernel, [f32(4, PART, WIDTH)], where, left, *by_x, *by_z)[0]


def far_sums(where_ref, left_ref, x_refs, z_refs, dz):
    acc = jnp.dot(left_of(where_ref, left_ref, 2, 0), x_refs[dz // 2][dz % 2],
                  preferred_element_type=jnp.float32)
    if dz == 2:
        for dx in range(4):
            acc += jnp.dot(left_of(where_ref, left_ref, dx, 1), z_refs[dx // 2][dx % 2],
                           preferred_element_type=jnp.float32)
    return grouped(acc)


def far(where, left, by_x, by_z, so_far):
    def kernel(where_ref, left_ref, xa, xb, za, zb, near_ref, out_ref):
        for dz in range(4):
            out_ref[dz] = near_ref[dz] + far_sums(where_ref, left_ref, (xa, xb), (za, zb), dz)

    return call(kernel, [f32(4, PART, WIDTH)], where, left, *by_x, *by_z, so_far)[0]


def far_and_first(where, left, by_x, by_z, so_far, own, ratio_rows):
    def kernel(where_ref, left_ref, xa, xb, za, zb, near_ref, own_ref, ratio_ref,
               sym_ref, visit_ref, send_ref, total_ref):
        z, c = where_ref[2], where_ref[3]
        for dz in range(4):
            mine = own_ref[dz]
            theirs = near_ref[dz] + far_sums(where_ref, left_ref, (xa, xb), (za, zb), dz)
            for core, part in ((c, mine), (1 - c, theirs)):
                g = lax.rem(z + 4 - dz, 4) * 2 + core
                sym_ref[:, pl.ds(pl.multiple_of(g * WIDTH, WIDTH), WIDTH)] = part[:WIDTH]
                frame = part[WIDTH:]
                visit_ref[pl.ds(g, 1), :] = jnp.sum(frame[:3], axis=0, keepdims=True)
                total_ref[pl.ds(g, 1), :] = jnp.sum(frame[:6], axis=0, keepdims=True)
        sums = row_parts(sym_ref, ratio_ref[...], visit_ref[...] / total_ref[...])
        send_ref[...] = jnp.broadcast_to(sums[None], send_ref.shape)

    out = [f32(WIDTH, COLS), f32(GROUPS, WIDTH), f32(128, 1, WIDTH), f32(GROUPS, WIDTH)]
    return call(kernel, out, where, left, *by_x, *by_z, so_far, own, ratio_rows)[:3]


def three_parts(v):
    hi = v.astype(jnp.bfloat16).astype(jnp.float32)
    mid = (v - hi).astype(jnp.bfloat16).astype(jnp.float32)
    return [hi, mid, v - hi - mid]


def prepare(where, blocks, frames):
    def kernel(where_ref, *refs):
        frame_ref, left_ref, visit_ref, ratio_ref, rows_ref = refs[4:]
        edge = jnp.zeros((TAU, WIDTH), jnp.bfloat16)
        rows_ref[:TAU, :] = edge
        rows_ref[TAU + FRAMES:, :] = edge
        for k in range(4):
            lo = lax.rem(where_ref[1] + k, 4) * BLOCK + TAU
            rows_ref[pl.ds(pl.multiple_of(lo, TAU), BLOCK), :] = refs[k][...]
        for lo in range(0, FRAMES + 2 * TAU, LANES):
            turned = rows_ref[lo:lo + LANES, :].astype(jnp.float32).T.astype(jnp.bfloat16)
            if lo < FRAMES:
                left_ref[:WIDTH, lo:lo + LANES] = turned
            if lo >= 2 * TAU:
                left_ref[WIDTH:2 * WIDTH, lo - 2 * TAU:lo - 2 * TAU + LANES] = turned
        total = [jnp.sum(frame_ref[32 * q:32 * q + 32].astype(jnp.float32), axis=0) for q in range(4)]
        total = jnp.concatenate([v[i:i + 1] for v in total for i in range(2)], axis=1)
        total = jnp.broadcast_to(total, (16, FRAMES))
        at = lax.broadcasted_iota(jnp.int32, (16, FRAMES), 1)
        line = lax.broadcasted_iota(jnp.int32, (16, FRAMES), 0)
        up = jnp.where(at < FRAMES - TAU, pltpu.roll(total, FRAMES - TAU, 1), 0.0)
        down = jnp.where(at >= TAU, pltpu.roll(total, TAU, 1), 0.0)
        weight = jnp.zeros((16, FRAMES), jnp.float32)
        for i, v in enumerate(three_parts(up) + three_parts(down)):
            weight = jnp.where(line == i, v, weight)
        left_ref[2 * WIDTH:, :] = weight.astype(jnp.bfloat16)
        weight = jnp.zeros((16, FRAMES), jnp.float32)
        for i, v in enumerate(three_parts(total)):
            weight = jnp.where(line == i, v, weight)
        weight = weight.astype(jnp.bfloat16)
        visit = jnp.sum(jnp.dot(weight, rows_ref[:FRAMES, :], preferred_element_type=jnp.float32),
                        axis=0, keepdims=True)
        back = jnp.sum(jnp.dot(weight, rows_ref[2 * TAU:, :], preferred_element_type=jnp.float32),
                       axis=0, keepdims=True)
        visit_ref[...] = visit
        ratio_ref[...] = jnp.broadcast_to(visit / (visit + back), (LANES, WIDTH)).T

    return pl.pallas_call(
        kernel,
        in_specs=[SMEM] + [VMEM] * 5,
        out_specs=[VMEM] * 3,
        out_shape=[jax.ShapeDtypeStruct((STACK, FRAMES), jnp.bfloat16), f32(1, WIDTH), f32(WIDTH, LANES)],
        scratch_shapes=[pltpu.VMEM((FRAMES + 2 * TAU, WIDTH), jnp.bfloat16)],
        compiler_params=pltpu.CompilerParams(vmem_limit_bytes=16 << 20),
    )(where, *[pltpu.with_memory_space_constraint(v, pltpu.VMEM) for v in blocks + [frames]])


def from_sides(v, axis):
    return [lax.ppermute(v, axis, along(k)) for k in (1, 3)]


def from_afar(where, sides, axis):
    def cut(_, back_ref, on_ref, first_ref, second_ref):
        first_ref[...] = back_ref[:2]
        second_ref[...] = on_ref[2:]

    half = jax.ShapeDtypeStruct((2,) + sides[0].shape[1:], sides[0].dtype)
    halves = call(cut, [half, half], where, *sides)
    return [lax.ppermute(halves[0], axis, along(1)), lax.ppermute(halves[1], axis, along(3))]


def swapped(vs):
    return [lax.ppermute(v, "c", [(0, 1), (1, 0)]) for v in vs]


def finish(where, got, last, sym, visit_cols, visit_rows):
    def kernel(where_ref, got_ref, last_ref, sym_ref, visit_col_ref, visit_row_ref,
               out_ref, share_ref, total_ref, row_ref, scale_ref, col_ref):
        step = pl.program_id(0)
        x, y, z, c = (where_ref[i] for i in range(4))

        @pl.when(step == 0)
        def _():
            w = (x * 4 + z) * 2 + c
            total_ref[...] = sum(last_ref[32 * k:32 * k + 32] for k in range(4))
            own = total_ref[w]
            scale_ref[...] = jnp.broadcast_to(STATES / own, (LANES, WIDTH)).T
            grand = jnp.sum(jnp.sum(total_ref[...], axis=0), axis=1, keepdims=True)
            share_ref[...] = STATES * own / grand
            total_ref[...] = sum(got_ref[32 * k:32 * k + 32] for k in range(4))
            row_ref[...] = jnp.broadcast_to(visit_row_ref[...] / total_ref[w], (LANES, WIDTH)).T
            for g in range(GROUPS):
                col_ref[g:g + 1, :] = visit_col_ref[g:g + 1, :] / total_ref[y * GROUPS + g]

        rows = pl.ds(pl.multiple_of(step * ROWS, ROWS), ROWS)
        for k in range(COLS // LANES):
            lo = k * LANES
            g, at = divmod(lo, WIDTH)
            out_ref[:, lo:lo + LANES] = scale_ref[rows, :] * sym_ref[:, lo:lo + LANES] / (
                row_ref[rows, :] + col_ref[g:g + 1, at:at + LANES])

    block = pl.BlockSpec((ROWS, COLS), lambda i: (i, 0))
    return pl.pallas_call(
        kernel,
        grid=(WIDTH // ROWS,),
        in_specs=[SMEM, VMEM, VMEM, block, VMEM, VMEM],
        out_specs=[block, pl.BlockSpec((1, WIDTH), lambda i: (0, 0))],
        out_shape=[f32(WIDTH, COLS), f32(1, WIDTH)],
        scratch_shapes=[pltpu.VMEM((32, 1, WIDTH), jnp.float32)]
        + [pltpu.VMEM((WIDTH, LANES), jnp.float32)] * 2 + [pltpu.VMEM((GROUPS, WIDTH), jnp.float32)],
        compiler_params=pltpu.CompilerParams(vmem_limit_bytes=16 << 20),
    )(where, got, last, sym, visit_cols, visit_rows)


def shards(member):
    x, y, z, c = (lax.axis_index(a) for a in ("x", "y", "z", "c"))
    where = jnp.stack([x, y, z, c])
    moved = lax.ppermute(member, ALL, across())
    part = jnp.sum(member, axis=1, dtype=jnp.float32)
    w, first = (v.astype(jnp.uint32) for v in ((x * 4 + z) * 2 + c, y * GROUPS))
    part, where, w, first = lax.optimization_barrier((part, where, w, first))
    frames = to_all(jnp.broadcast_to(part.astype(jnp.bfloat16).reshape(2, WIDTH), (128, 2, WIDTH)))
    once_x = jnp.stack(ring(moved[:FIRST], "z"))
    once_z = jnp.stack(ring(moved[FIRST:], "x"))
    near_x = from_sides(once_x, "x")
    near_z = from_sides(once_z, "z")
    far_x = from_afar(where, near_x, "x")
    far_z = from_afar(where, near_z, "z")
    kept, frames = lax.optimization_barrier((member, frames))
    blocks = [member] + [lax.ppermute(kept, "y", along(-k)) for k in (1, 2, 3)]
    left, visit_rows, ratio_rows = prepare(where, blocks, frames)
    own = near(where, left, [once_x] + near_x, [once_z] + near_z)
    once_x, once_z = swapped([once_x, once_z])
    near_x, near_z = swapped(near_x), swapped(near_z)
    sibling = near(where, left, [once_x] + near_x, [once_z] + near_z)
    own = far(where, left, far_x, far_z, own)
    far_x, far_z = swapped(far_x), swapped(far_z)
    sym, visit_cols, send = far_and_first(where, left, far_x, far_z, sibling, own, ratio_rows)
    for _ in range(2):
        got = to_all(send)
        totals = jnp.sum(got.reshape(4, 32, WIDTH), axis=0)
        total_rows = lax.dynamic_slice(totals, (w, jnp.uint32(0)), (1, WIDTH)).reshape(WIDTH)
        total_cols = lax.dynamic_slice(totals, (first, jnp.uint32(0)), (GROUPS, WIDTH))
        ratio_rows = visit_rows.reshape(WIDTH) / total_rows
        ratio = ratio_rows[:, None] + (visit_cols / total_cols).reshape(COLS)[None, :]
        send = jnp.broadcast_to(jnp.sum(sym / ratio, axis=1), (128, 1, WIDTH))
    transition, stationary = finish(where, got, to_all(send), sym, visit_cols, visit_rows)
    return (transition, stationary.reshape(WIDTH))


def solution(mesh):
    mesh = Mesh(mesh.devices.reshape(4, 4, 2, 4), ALL)
    return jax.shard_map(
        shards,
        mesh=mesh,
        in_specs=(P("y", WIDE),),
        out_specs=(P(WIDE, "y"), P(WIDE)),
        check_vma=False,
    )
```

```python
import jax
import jax.numpy as jnp
from jax import lax
from jax.experimental import pallas as pl
from jax.experimental.pallas import tpu as pltpu
from jax.sharding import Mesh, PartitionSpec as P


STATES = 8192
TAU = 64
FRAMES = 2048
WIDE = ("x", "z", "c")
ALL = ("x", "z", "c", "y")
BLOCK = 512
WIDTH = 256
COLS = 2048
GROUPS = COLS // WIDTH
FIRST = 256
STACK = 2 * WIDTH + 16
PART = WIDTH + 16
LANES = 128
ROWS = 64


def place(x, y, z, c):
    return ((x * 4 + z) * 2 + c) * 4 + y


def across():
    return [
        (place(x, y, z, c), place(y, x, z, c))
        for x in range(4) for y in range(4) for z in range(4) for c in range(2)
    ]


def along(k):
    return [(i, (i + k) % 4) for i in range(4)]


def ring(v, axis):
    return [v] + [lax.ppermute(v, axis, along(k)) for k in (1, 2, 3)]


def to_all(sent):
    return lax.all_to_all(sent, ("y",) + WIDE, 0, 0)


VMEM = pl.BlockSpec(memory_space=pltpu.VMEM)
SMEM = pl.BlockSpec(memory_space=pltpu.SMEM)


def f32(*shape):
    return jax.ShapeDtypeStruct(shape, jnp.float32)


def row_parts(sym_ref, ratio_rows, ratio_cols):
    parts = []
    for top in range(0, WIDTH, 64):
        acc = jnp.zeros((64, LANES), jnp.float32)
        for k in range(COLS // LANES):
            g, lo = divmod(k * LANES, WIDTH)
            acc += sym_ref[top:top + 64, k * LANES:(k + 1) * LANES] / (
                ratio_rows[top:top + 64] + ratio_cols[g:g + 1, lo:lo + LANES])
        parts.append(acc)
    return jnp.sum(jnp.concatenate(parts, axis=0).T, axis=0, keepdims=True)


def grouped(acc):
    return jnp.concatenate([acc[:WIDTH] + acc[WIDTH:2 * WIDTH], acc[2 * WIDTH:]], axis=0)


def call(kernel, out, *operands):
    return pl.pallas_call(
        kernel,
        in_specs=[SMEM] + [VMEM] * (len(operands) - 1),
        out_specs=[VMEM] * len(out),
        out_shape=out,
        compiler_params=pltpu.CompilerParams(vmem_limit_bytes=16 << 20),
    )(operands[0], *[pltpu.with_memory_space_constraint(v, pltpu.VMEM) for v in operands[1:]])


def left_of(where_ref, left_ref, back, late):
    lo = lax.rem(where_ref[late] + 4 - back, 4) * BLOCK + late * FIRST
    return left_ref[:, pl.ds(pl.multiple_of(lo, FIRST), FIRST)]


NEAR = (0, 1, 3)


def near(where, left, by_x, by_z):
    def kernel(where_ref, left_ref, *refs):
        x_refs, z_refs, out_ref = refs[:3], refs[3:6], refs[6]
        for dz in range(4):
            acc = jnp.zeros((STACK, WIDTH), jnp.float32)
            for i, dx in enumerate(NEAR):
                acc += jnp.dot(left_of(where_ref, left_ref, dx, 0), x_refs[i][dz],
                               preferred_element_type=jnp.float32)
            if dz in NEAR:
                for dy in range(4):
                    acc += jnp.dot(left_of(where_ref, left_ref, dy, 1), z_refs[NEAR.index(dz)][dy],
                                   preferred_element_type=jnp.float32)
            out_ref[dz] = grouped(acc)

    return call(kernel, [f32(4, PART, WIDTH)], where, left, *by_x, *by_z)[0]


def far_sums(where_ref, left_ref, x_refs, z_refs, dz):
    acc = jnp.dot(left_of(where_ref, left_ref, 2, 0), x_refs[dz // 2][dz % 2],
                  preferred_element_type=jnp.float32)
    if dz == 2:
        for dy in range(4):
            acc += jnp.dot(left_of(where_ref, left_ref, dy, 1), z_refs[dy // 2][dy % 2],
                           preferred_element_type=jnp.float32)
    return grouped(acc)


def far(where, left, by_x, by_z, so_far):
    def kernel(where_ref, left_ref, xa, xb, za, zb, near_ref, out_ref):
        for dz in range(4):
            out_ref[dz] = near_ref[dz] + far_sums(where_ref, left_ref, (xa, xb), (za, zb), dz)

    return call(kernel, [f32(4, PART, WIDTH)], where, left, *by_x, *by_z, so_far)[0]


def far_and_first(where, left, by_x, by_z, so_far, own, ratio_rows):
    def kernel(where_ref, left_ref, xa, xb, za, zb, near_ref, own_ref, ratio_ref,
               sym_ref, visit_ref, send_ref, total_ref):
        z, c = where_ref[2], where_ref[3]
        for dz in range(4):
            mine = own_ref[dz]
            theirs = near_ref[dz] + far_sums(where_ref, left_ref, (xa, xb), (za, zb), dz)
            for core, part in ((c, mine), (1 - c, theirs)):
                g = lax.rem(z + 4 - dz, 4) * 2 + core
                sym_ref[:, pl.ds(pl.multiple_of(g * WIDTH, WIDTH), WIDTH)] = part[:WIDTH]
                frame = part[WIDTH:]
                visit_ref[pl.ds(g, 1), :] = jnp.sum(frame[:3], axis=0, keepdims=True)
                total_ref[pl.ds(g, 1), :] = jnp.sum(frame[:6], axis=0, keepdims=True)
        sums = row_parts(sym_ref, ratio_ref[...], visit_ref[...] / total_ref[...])
        send_ref[...] = jnp.broadcast_to(sums[None], send_ref.shape)

    out = [f32(WIDTH, COLS), f32(GROUPS, WIDTH), f32(128, 1, WIDTH), f32(GROUPS, WIDTH)]
    return call(kernel, out, where, left, *by_x, *by_z, so_far, own, ratio_rows)[:3]


def three_parts(v):
    hi = v.astype(jnp.bfloat16).astype(jnp.float32)
    mid = (v - hi).astype(jnp.bfloat16).astype(jnp.float32)
    return [hi, mid, v - hi - mid]


def prepare(where, blocks, frames):
    def kernel(where_ref, *refs):
        frame_ref, left_ref, visit_ref, ratio_ref, rows_ref = refs[4:]
        edge = jnp.zeros((TAU, WIDTH), jnp.bfloat16)
        rows_ref[:TAU, :] = edge
        rows_ref[TAU + FRAMES:, :] = edge
        for k in range(4):
            lo = lax.rem(where_ref[1] + k, 4) * BLOCK + TAU
            rows_ref[pl.ds(pl.multiple_of(lo, TAU), BLOCK), :] = refs[k][...]
        for lo in range(0, FRAMES + 2 * TAU, LANES):
            turned = rows_ref[lo:lo + LANES, :].astype(jnp.float32).T.astype(jnp.bfloat16)
            if lo < FRAMES:
                left_ref[:WIDTH, lo:lo + LANES] = turned
            if lo >= 2 * TAU:
                left_ref[WIDTH:2 * WIDTH, lo - 2 * TAU:lo - 2 * TAU + LANES] = turned
        total = [jnp.sum(frame_ref[32 * q:32 * q + 32].astype(jnp.float32), axis=0) for q in range(4)]
        total = jnp.concatenate([v[i:i + 1] for v in total for i in range(2)], axis=1)
        total = jnp.broadcast_to(total, (16, FRAMES))
        at = lax.broadcasted_iota(jnp.int32, (16, FRAMES), 1)
        line = lax.broadcasted_iota(jnp.int32, (16, FRAMES), 0)
        up = jnp.where(at < FRAMES - TAU, pltpu.roll(total, FRAMES - TAU, 1), 0.0)
        down = jnp.where(at >= TAU, pltpu.roll(total, TAU, 1), 0.0)
        weight = jnp.zeros((16, FRAMES), jnp.float32)
        for i, v in enumerate(three_parts(up) + three_parts(down)):
            weight = jnp.where(line == i, v, weight)
        left_ref[2 * WIDTH:, :] = weight.astype(jnp.bfloat16)
        weight = jnp.zeros((16, FRAMES), jnp.float32)
        for i, v in enumerate(three_parts(total)):
            weight = jnp.where(line == i, v, weight)
        weight = weight.astype(jnp.bfloat16)
        visit = jnp.sum(jnp.dot(weight, rows_ref[:FRAMES, :], preferred_element_type=jnp.float32),
                        axis=0, keepdims=True)
        back = jnp.sum(jnp.dot(weight, rows_ref[2 * TAU:, :], preferred_element_type=jnp.float32),
                       axis=0, keepdims=True)
        visit_ref[...] = visit
        ratio_ref[...] = jnp.broadcast_to(visit / (visit + back), (LANES, WIDTH)).T

    return pl.pallas_call(
        kernel,
        in_specs=[SMEM] + [VMEM] * 5,
        out_specs=[VMEM] * 3,
        out_shape=[jax.ShapeDtypeStruct((STACK, FRAMES), jnp.bfloat16), f32(1, WIDTH), f32(WIDTH, LANES)],
        scratch_shapes=[pltpu.VMEM((FRAMES + 2 * TAU, WIDTH), jnp.bfloat16)],
        compiler_params=pltpu.CompilerParams(vmem_limit_bytes=16 << 20),
    )(where, *[pltpu.with_memory_space_constraint(v, pltpu.VMEM) for v in blocks + [frames]])


def from_sides(v, axis):
    return [lax.ppermute(v, axis, along(k)) for k in (1, 3)]


def from_afar(where, sides, axis):
    def cut(_, back_ref, on_ref, first_ref, second_ref):
        first_ref[...] = back_ref[:2]
        second_ref[...] = on_ref[2:]

    half = jax.ShapeDtypeStruct((2,) + sides[0].shape[1:], sides[0].dtype)
    halves = call(cut, [half, half], where, *sides)
    return [lax.ppermute(halves[0], axis, along(1)), lax.ppermute(halves[1], axis, along(3))]


def swapped(vs):
    return [lax.ppermute(v, "c", [(0, 1), (1, 0)]) for v in vs]


def finish(where, got, last, sym, visit_cols, visit_rows):
    def kernel(where_ref, got_ref, last_ref, sym_ref, visit_col_ref, visit_row_ref,
               out_ref, share_ref, total_ref, row_ref, scale_ref, col_ref):
        step = pl.program_id(0)
        x, y, z, c = (where_ref[i] for i in range(4))

        @pl.when(step == 0)
        def _():
            w = (x * 4 + z) * 2 + c
            total_ref[...] = sum(last_ref[32 * k:32 * k + 32] for k in range(4))
            own = total_ref[w]
            scale_ref[...] = jnp.broadcast_to(STATES / own, (LANES, WIDTH)).T
            grand = jnp.sum(jnp.sum(total_ref[...], axis=0), axis=1, keepdims=True)
            share_ref[...] = STATES * own / grand
            total_ref[...] = sum(got_ref[32 * k:32 * k + 32] for k in range(4))
            row_ref[...] = jnp.broadcast_to(visit_row_ref[...] / total_ref[w], (LANES, WIDTH)).T
            for g in range(GROUPS):
                col_ref[g:g + 1, :] = visit_col_ref[g:g + 1, :] / total_ref[y * GROUPS + g]

        rows = pl.ds(pl.multiple_of(step * ROWS, ROWS), ROWS)
        for k in range(COLS // LANES):
            lo = k * LANES
            g, at = divmod(lo, WIDTH)
            out_ref[:, lo:lo + LANES] = scale_ref[rows, :] * sym_ref[:, lo:lo + LANES] / (
                row_ref[rows, :] + col_ref[g:g + 1, at:at + LANES])

    block = pl.BlockSpec((ROWS, COLS), lambda i: (i, 0))
    return pl.pallas_call(
        kernel,
        grid=(WIDTH // ROWS,),
        in_specs=[SMEM, VMEM, VMEM, block, VMEM, VMEM],
        out_specs=[block, pl.BlockSpec((1, WIDTH), lambda i: (0, 0))],
        out_shape=[f32(WIDTH, COLS), f32(1, WIDTH)],
        scratch_shapes=[pltpu.VMEM((32, 1, WIDTH), jnp.float32)]
        + [pltpu.VMEM((WIDTH, LANES), jnp.float32)] * 2 + [pltpu.VMEM((GROUPS, WIDTH), jnp.float32)],
        compiler_params=pltpu.CompilerParams(vmem_limit_bytes=16 << 20),
    )(where, got, last, sym, visit_cols, visit_rows)


def shards(member):
    x, y, z, c = (lax.axis_index(a) for a in ("x", "y", "z", "c"))
    where = jnp.stack([x, y, z, c])
    moved = lax.ppermute(member[:FIRST], ALL, across())
    part = jnp.sum(member, axis=1, dtype=jnp.float32)
    w, first = (v.astype(jnp.uint32) for v in ((x * 4 + z) * 2 + c, y * GROUPS))
    part, where, w, first = lax.optimization_barrier((part, where, w, first))
    frames = to_all(jnp.broadcast_to(part.astype(jnp.bfloat16).reshape(2, WIDTH), (128, 2, WIDTH)))
    planes = jnp.stack(ring(member[FIRST:], "x"))
    once_x = jnp.stack(ring(moved, "z"))
    leave = [lax.dynamic_index_in_dim(planes, lax.rem(x + 8 - y - k, 4), 0, False) for k in range(4)]
    once_z = jnp.stack([leave[0]] + [lax.ppermute(leave[k], "y", along(k)) for k in (1, 2, 3)])
    near_x = from_sides(once_x, "x")
    near_z = from_sides(once_z, "z")
    far_x = from_afar(where, near_x, "x")
    far_z = from_afar(where, near_z, "z")
    kept, frames = lax.optimization_barrier((member, frames))
    blocks = [member] + [lax.ppermute(kept, "y", along(-k)) for k in (1, 2, 3)]
    left, visit_rows, ratio_rows = prepare(where, blocks, frames)
    own = near(where, left, [once_x] + near_x, [once_z] + near_z)
    once_x, once_z = swapped([once_x, once_z])
    near_x, near_z = swapped(near_x), swapped(near_z)
    sibling = near(where, left, [once_x] + near_x, [once_z] + near_z)
    own = far(where, left, far_x, far_z, own)
    far_x, far_z = swapped(far_x), swapped(far_z)
    sym, visit_cols, send = far_and_first(where, left, far_x, far_z, sibling, own, ratio_rows)
    for _ in range(2):
        got = to_all(send)
        totals = jnp.sum(got.reshape(4, 32, WIDTH), axis=0)
        total_rows = lax.dynamic_slice(totals, (w, jnp.uint32(0)), (1, WIDTH)).reshape(WIDTH)
        total_cols = lax.dynamic_slice(totals, (first, jnp.uint32(0)), (GROUPS, WIDTH))
        ratio_rows = visit_rows.reshape(WIDTH) / total_rows
        ratio = ratio_rows[:, None] + (visit_cols / total_cols).reshape(COLS)[None, :]
        send = jnp.broadcast_to(jnp.sum(sym / ratio, axis=1), (128, 1, WIDTH))
    transition, stationary = finish(where, got, to_all(send), sym, visit_cols, visit_rows)
    return (transition, stationary.reshape(WIDTH))


def solution(mesh):
    mesh = Mesh(mesh.devices.reshape(4, 4, 2, 4), ALL)
    return jax.shard_map(
        shards,
        mesh=mesh,
        in_specs=(P("y", WIDE),),
        out_specs=(P(WIDE, "y"), P(WIDE)),
        check_vma=False,
    )
```

```python
import jax
import jax.numpy as jnp
from jax import lax
from jax.experimental import pallas as pl
from jax.experimental.pallas import tpu as pltpu
from jax.sharding import Mesh, PartitionSpec as P


STATES = 8192
TAU = 64
FRAMES = 2048
WIDE = ("x", "z", "c")
ALL = ("x", "z", "c", "y")
BLOCK = 512
WIDTH = 256
COLS = 2048
GROUPS = COLS // WIDTH
FIRST = 256
STACK = 2 * WIDTH + 16
PART = WIDTH + 16
LANES = 128
ROWS = 64


def place(x, y, z, c):
    return ((x * 4 + z) * 2 + c) * 4 + y


def across():
    return [
        (place(x, y, z, c), place(y, x, z, c))
        for x in range(4) for y in range(4) for z in range(4) for c in range(2)
    ]


def along(k):
    return [(i, (i + k) % 4) for i in range(4)]


def ring(v, axis):
    return [v] + [lax.ppermute(v, axis, along(k)) for k in (1, 2, 3)]


def to_all(sent):
    return lax.all_to_all(sent, ("y",) + WIDE, 0, 0)


VMEM = pl.BlockSpec(memory_space=pltpu.VMEM)
SMEM = pl.BlockSpec(memory_space=pltpu.SMEM)


def f32(*shape):
    return jax.ShapeDtypeStruct(shape, jnp.float32)


def row_parts(sym_ref, ratio_rows, ratio_cols):
    parts = []
    for top in range(0, WIDTH, 64):
        acc = jnp.zeros((64, LANES), jnp.float32)
        for k in range(COLS // LANES):
            g, lo = divmod(k * LANES, WIDTH)
            acc += sym_ref[top:top + 64, k * LANES:(k + 1) * LANES] / (
                ratio_rows[top:top + 64] + ratio_cols[g:g + 1, lo:lo + LANES])
        parts.append(acc)
    return jnp.sum(jnp.concatenate(parts, axis=0).T, axis=0, keepdims=True)


def grouped(acc):
    return jnp.concatenate([acc[:WIDTH] + acc[WIDTH:2 * WIDTH], acc[2 * WIDTH:]], axis=0)


def call(kernel, out, *operands):
    return pl.pallas_call(
        kernel,
        in_specs=[SMEM] + [VMEM] * (len(operands) - 1),
        out_specs=[VMEM] * len(out),
        out_shape=out,
        compiler_params=pltpu.CompilerParams(vmem_limit_bytes=16 << 20),
    )(operands[0], *[pltpu.with_memory_space_constraint(v, pltpu.VMEM) for v in operands[1:]])


def left_of(where_ref, left_ref, dx, late):
    lo = lax.rem(where_ref[0] + 4 - dx, 4) * BLOCK + late * FIRST
    return left_ref[:, pl.ds(pl.multiple_of(lo, FIRST), FIRST)]


NEAR = (0, 1, 3)


def near(where, left, by_x, by_z):
    def kernel(where_ref, left_ref, *refs):
        x_refs, z_refs, out_ref = refs[:3], refs[3:6], refs[6]
        for dz in range(4):
            acc = jnp.zeros((STACK, WIDTH), jnp.float32)
            for i, dx in enumerate(NEAR):
                acc += jnp.dot(left_of(where_ref, left_ref, dx, 0), x_refs[i][dz],
                               preferred_element_type=jnp.float32)
            if dz in NEAR:
                for dx in range(4):
                    acc += jnp.dot(left_of(where_ref, left_ref, dx, 1), z_refs[NEAR.index(dz)][dx],
                                   preferred_element_type=jnp.float32)
            out_ref[dz] = grouped(acc)

    return call(kernel, [f32(4, PART, WIDTH)], where, left, *by_x, *by_z)[0]


def far_sums(where_ref, left_ref, x_refs, z_refs, dz):
    acc = jnp.dot(left_of(where_ref, left_ref, 2, 0), x_refs[dz // 2][dz % 2],
                  preferred_element_type=jnp.float32)
    if dz == 2:
        for dx in range(4):
            acc += jnp.dot(left_of(where_ref, left_ref, dx, 1), z_refs[dx // 2][dx % 2],
                           preferred_element_type=jnp.float32)
    return grouped(acc)


def far_and_first(where, left, own, sibling, ratio_rows):
    def kernel(where_ref, left_ref, *refs):
        ratio_ref, sym_ref, visit_ref, send_ref, total_ref = refs[10:]
        z, c = where_ref[2], where_ref[3]
        for core, (near_ref, xa, xb, za, zb) in ((c, refs[:5]), (1 - c, refs[5:10])):
            for dz in range(4):
                part = near_ref[dz] + far_sums(where_ref, left_ref, (xa, xb), (za, zb), dz)
                g = lax.rem(z + 4 - dz, 4) * 2 + core
                sym_ref[:, pl.ds(pl.multiple_of(g * WIDTH, WIDTH), WIDTH)] = part[:WIDTH]
                frame = part[WIDTH:]
                visit_ref[pl.ds(g, 1), :] = jnp.sum(frame[:3], axis=0, keepdims=True)
                total_ref[pl.ds(g, 1), :] = jnp.sum(frame[:6], axis=0, keepdims=True)
        sums = row_parts(sym_ref, ratio_ref[...], visit_ref[...] / total_ref[...])
        send_ref[...] = jnp.broadcast_to(sums[None], send_ref.shape)

    out = [f32(WIDTH, COLS), f32(GROUPS, WIDTH), f32(128, 1, WIDTH), f32(GROUPS, WIDTH)]
    return call(kernel, out, where, left, *own, *sibling, ratio_rows)[:3]


def three_parts(v):
    hi = v.astype(jnp.bfloat16).astype(jnp.float32)
    mid = (v - hi).astype(jnp.bfloat16).astype(jnp.float32)
    return [hi, mid, v - hi - mid]


def prepare(where, blocks, frames):
    def kernel(where_ref, *refs):
        frame_ref, left_ref, visit_ref, ratio_ref, rows_ref = refs[4:]
        edge = jnp.zeros((TAU, WIDTH), jnp.bfloat16)
        rows_ref[:TAU, :] = edge
        rows_ref[TAU + FRAMES:, :] = edge
        for k in range(4):
            lo = lax.rem(where_ref[1] + k, 4) * BLOCK + TAU
            rows_ref[pl.ds(pl.multiple_of(lo, TAU), BLOCK), :] = refs[k][...]
        for lo in range(0, FRAMES + 2 * TAU, LANES):
            turned = rows_ref[lo:lo + LANES, :].astype(jnp.float32).T.astype(jnp.bfloat16)
            if lo < FRAMES:
                left_ref[:WIDTH, lo:lo + LANES] = turned
            if lo >= 2 * TAU:
                left_ref[WIDTH:2 * WIDTH, lo - 2 * TAU:lo - 2 * TAU + LANES] = turned
        total = [jnp.sum(frame_ref[32 * q:32 * q + 32].astype(jnp.float32), axis=0) for q in range(4)]
        total = jnp.concatenate([v[i:i + 1] for v in total for i in range(2)], axis=1)
        total = jnp.broadcast_to(total, (16, FRAMES))
        at = lax.broadcasted_iota(jnp.int32, (16, FRAMES), 1)
        line = lax.broadcasted_iota(jnp.int32, (16, FRAMES), 0)
        up = jnp.where(at < FRAMES - TAU, pltpu.roll(total, FRAMES - TAU, 1), 0.0)
        down = jnp.where(at >= TAU, pltpu.roll(total, TAU, 1), 0.0)
        weight = jnp.zeros((16, FRAMES), jnp.float32)
        for i, v in enumerate(three_parts(up) + three_parts(down)):
            weight = jnp.where(line == i, v, weight)
        left_ref[2 * WIDTH:, :] = weight.astype(jnp.bfloat16)
        weight = jnp.zeros((16, FRAMES), jnp.float32)
        for i, v in enumerate(three_parts(total)):
            weight = jnp.where(line == i, v, weight)
        weight = weight.astype(jnp.bfloat16)
        visit = jnp.sum(jnp.dot(weight, rows_ref[:FRAMES, :], preferred_element_type=jnp.float32),
                        axis=0, keepdims=True)
        back = jnp.sum(jnp.dot(weight, rows_ref[2 * TAU:, :], preferred_element_type=jnp.float32),
                       axis=0, keepdims=True)
        visit_ref[...] = visit
        ratio_ref[...] = jnp.broadcast_to(visit / (visit + back), (LANES, WIDTH)).T

    return pl.pallas_call(
        kernel,
        in_specs=[SMEM] + [VMEM] * 5,
        out_specs=[VMEM] * 3,
        out_shape=[jax.ShapeDtypeStruct((STACK, FRAMES), jnp.bfloat16), f32(1, WIDTH), f32(WIDTH, LANES)],
        scratch_shapes=[pltpu.VMEM((FRAMES + 2 * TAU, WIDTH), jnp.bfloat16)],
        compiler_params=pltpu.CompilerParams(vmem_limit_bytes=16 << 20),
    )(where, *[pltpu.with_memory_space_constraint(v, pltpu.VMEM) for v in blocks + [frames]])


def from_sides(v, axis):
    return [lax.ppermute(v, axis, along(k)) for k in (1, 3)]


def from_afar(where, sides, axis):
    def cut(_, back_ref, on_ref, first_ref, second_ref):
        first_ref[...] = back_ref[:2]
        second_ref[...] = on_ref[2:]

    half = jax.ShapeDtypeStruct((2,) + sides[0].shape[1:], sides[0].dtype)
    halves = call(cut, [half, half], where, *sides)
    return [lax.ppermute(halves[0], axis, along(1)), lax.ppermute(halves[1], axis, along(3))]


def swapped(vs):
    return [lax.ppermute(v, "c", [(0, 1), (1, 0)]) for v in vs]


def finish(where, last, sym, ratio_rows, ratio_cols):
    def kernel(where_ref, last_ref, sym_ref, ratio_ref, col_ref,
               out_ref, share_ref, total_ref, row_ref, scale_ref):
        step = pl.program_id(0)
        x, _, z, c = (where_ref[i] for i in range(4))

        @pl.when(step == 0)
        def _():
            total_ref[...] = sum(last_ref[32 * k:32 * k + 32] for k in range(4))
            own = total_ref[(x * 4 + z) * 2 + c]
            scale_ref[...] = jnp.broadcast_to(STATES / own, (LANES, WIDTH)).T
            grand = jnp.sum(jnp.sum(total_ref[...], axis=0), axis=1, keepdims=True)
            share_ref[...] = STATES * own / grand
            row_ref[...] = jnp.broadcast_to(ratio_ref[...], (LANES, WIDTH)).T

        rows = pl.ds(pl.multiple_of(step * ROWS, ROWS), ROWS)
        for k in range(COLS // LANES):
            lo = k * LANES
            g, at = divmod(lo, WIDTH)
            out_ref[:, lo:lo + LANES] = scale_ref[rows, :] * sym_ref[:, lo:lo + LANES] / (
                row_ref[rows, :] + col_ref[g:g + 1, at:at + LANES])

    block = pl.BlockSpec((ROWS, COLS), lambda i: (i, 0))
    return pl.pallas_call(
        kernel,
        grid=(WIDTH // ROWS,),
        in_specs=[SMEM, VMEM, block, VMEM, VMEM],
        out_specs=[block, pl.BlockSpec((1, WIDTH), lambda i: (0, 0))],
        out_shape=[f32(WIDTH, COLS), f32(1, WIDTH)],
        scratch_shapes=[pltpu.VMEM((32, 1, WIDTH), jnp.float32)]
        + [pltpu.VMEM((WIDTH, LANES), jnp.float32)] * 2,
        compiler_params=pltpu.CompilerParams(vmem_limit_bytes=16 << 20),
    )(where, last, sym, ratio_rows, ratio_cols)


def shards(member):
    x, y, z, c = (lax.axis_index(a) for a in ("x", "y", "z", "c"))
    where = jnp.stack([x, y, z, c])
    moved = lax.ppermute(member, ALL, across())
    part = jnp.sum(member, axis=1, dtype=jnp.float32)
    w, first = (v.astype(jnp.uint32) for v in ((x * 4 + z) * 2 + c, y * GROUPS))
    part, where, w, first = lax.optimization_barrier((part, where, w, first))
    frames = to_all(jnp.broadcast_to(part.astype(jnp.bfloat16).reshape(2, WIDTH), (128, 2, WIDTH)))
    once_x = jnp.stack(ring(moved[:FIRST], "z"))
    once_z = jnp.stack(ring(moved[FIRST:], "x"))
    near_x = from_sides(once_x, "x")
    near_z = from_sides(once_z, "z")
    far_x = from_afar(where, near_x, "x")
    far_z = from_afar(where, near_z, "z")
    kept, frames = lax.optimization_barrier((member, frames))
    blocks = [member] + [lax.ppermute(kept, "y", along(-k)) for k in (1, 2, 3)]
    left, visit_rows, ratio_rows = prepare(where, blocks, frames)
    own = near(where, left, [once_x] + near_x, [once_z] + near_z)
    once_x, once_z = swapped([once_x, once_z])
    near_x, near_z = swapped(near_x), swapped(near_z)
    sibling = near(where, left, [once_x] + near_x, [once_z] + near_z)
    own, sibling = [own, *far_x, *far_z], [sibling, *swapped(far_x + far_z)]
    sym, visit_cols, send = far_and_first(where, left, own, sibling, ratio_rows)
    for _ in range(2):
        got = to_all(send)
        totals = jnp.sum(got.reshape(4, 32, WIDTH), axis=0)
        total_rows = lax.dynamic_slice(totals, (w, jnp.uint32(0)), (1, WIDTH)).reshape(WIDTH)
        total_cols = lax.dynamic_slice(totals, (first, jnp.uint32(0)), (GROUPS, WIDTH))
        ratio_rows = visit_rows.reshape(WIDTH) / total_rows
        ratio_cols = visit_cols / total_cols
        ratio = ratio_rows[:, None] + ratio_cols.reshape(COLS)[None, :]
        send = jnp.broadcast_to(jnp.sum(sym / ratio, axis=1), (128, 1, WIDTH))
    transition, stationary = finish(where, to_all(send), sym, ratio_rows.reshape(1, WIDTH), ratio_cols)
    return (transition, stationary.reshape(WIDTH))


def solution(mesh):
    mesh = Mesh(mesh.devices.reshape(4, 4, 2, 4), ALL)
    return jax.shard_map(
        shards,
        mesh=mesh,
        in_specs=(P("y", WIDE),),
        out_specs=(P(WIDE, "y"), P(WIDE)),
        check_vma=False,
    )
```
